32 devices in a mesh: fsdp: 8 (over y, x, core), tp: 4 (over z).
Axes of the slice: x: 2, y: 2, z: 4, core: 2. Of those that a mesh axis runs over, the one named last changes fastest.
Arguments:
- tokens: bfloat16 [8192, 768], P(('fsdp', 'tp')), may hold values from -6 to 6
- cotangent: bfloat16 [8192, 768], P(('fsdp', 'tp')), may hold values from -6 to 6
- seq_lengths: int32 [8], P('fsdp'), may hold values from 256 to 1024, as said below
- expert_routes: int32 [8192, 2], P('fsdp'), may hold values from 0 to 7, as said below
- expert_slots: int32 [8192, 2], P('fsdp'), may hold values from 0 to 319, as said below
- attn_gain: bfloat16 [768], P(('fsdp', 'tp')), may hold values from 0.5 to 1.5
- ffn_gain: bfloat16 [768], P(('fsdp', 'tp')), may hold values from 0.5 to 1.5
- router_weight: bfloat16 [768, 8], P(('fsdp', 'tp')), may hold values from -0.15625 to 0.15625
- query_weight: bfloat16 [768, 768], P('fsdp', 'tp'), may hold values from -0.21875 to 0.21875
- key_weight: bfloat16 [768, 768], P('fsdp', 'tp'), may hold values from -0.21875 to 0.21875
- value_weight: bfloat16 [768, 768], P('fsdp', 'tp'), may hold values from -0.21875 to 0.21875
- out_weight: bfloat16 [768, 768], P('tp', 'fsdp'), may hold values from -1.25 to 1.25
- shared_gate: bfloat16 [768, 2048], P('fsdp', 'tp'), may hold values from -0.21875 to 0.21875
- shared_up: bfloat16 [768, 2048], P('fsdp', 'tp'), may hold values from -0.21875 to 0.21875
- shared_down: bfloat16 [2048, 768], P('tp', 'fsdp'), may hold values from -0.125 to 0.125
- expert_gate: bfloat16 [8, 768, 2048], P(None, 'fsdp', 'tp'), may hold values from -0.21875 to 0.21875
- expert_up: bfloat16 [8, 768, 2048], P(None, 'fsdp', 'tp'), may hold values from -0.21875 to 0.21875
- expert_down: bfloat16 [8, 2048, 768], P(None, 'tp', 'fsdp'), may hold values from -0.125 to 0.125
Outputs:
- layer_out: bfloat16 [8192, 768], P(('fsdp', 'tp'))
- d_tokens: float32 [8192, 768], P(('fsdp', 'tp'))
- d_attn_gain: float32 [768], P(('fsdp', 'tp'))
- d_ffn_gain: float32 [768], P(('fsdp', 'tp'))
- d_router_weight: float32 [768, 8], P(('fsdp', 'tp'))
- d_query_weight: float32 [768, 768], P('fsdp', 'tp')
- d_key_weight: float32 [768, 768], P('fsdp', 'tp')
- d_value_weight: float32 [768, 768], P('fsdp', 'tp')
- d_out_weight: float32 [768, 768], P('tp', 'fsdp')
- d_shared_gate: float32 [768, 2048], P('fsdp', 'tp')
- d_shared_up: float32 [768, 2048], P('fsdp', 'tp')
- d_shared_down: float32 [2048, 768], P('tp', 'fsdp')
- d_expert_gate: float32 [8, 768, 2048], P(None, 'fsdp', 'tp')
- d_expert_up: float32 [8, 768, 2048], P(None, 'fsdp', 'tp')
- d_expert_down: float32 [8, 2048, 768], P(None, 'tp', 'fsdp')
The draws below stay inside these ranges and needn't reach their ends.
Inputs may be any that keep to these rules, and one draw needn't show every extreme that they name: `seq_lengths`: some sequence has exactly 1024 live tokens. `expert_routes`: within each group of 1024 tokens a token's two experts differ, each expert receives at most 320 of the 2048 picks, and some expert receives exactly 320. `expert_slots`: within each group of 1024 tokens the pairs (expert, slot) of all picks differ; an expert with n picks in the group uses slots 0 to n - 1.
All inputs are finite; a program needn't handle non-finite values.
Results may differ from the reference program's by a relative error of at most 0.018.
Values may be sent and summed in bfloat16 or wider, within the bound.
No kernel may reach another device: no remote copies, remote signals or barrier semaphores. Data moves between devices by JAX's collectives and lax.ppermute only.
A program may use at most 192 MiB of HBM per device.

```python
import jax
import jax.numpy as jnp
from jax import lax

D = 768
HEADS = 12
HD = 64
FF = 2048
FFS = 2048
EXPERTS = 8
LEN = 1024
SEQ_GRP = 1
GROUP = 1024
CAP = 320
ATT = 768
SEQS = 8
TOKENS = 8192


def route_table(base_key):
    groups = TOKENS // GROUP
    pick_count = 2 * GROUP
    mean_load = pick_count // EXPERTS
    headroom = CAP - mean_load

    def one_group(group_key):
        subkeys = jax.random.split(group_key, 5)
        pairing = jax.random.permutation(subkeys[0], EXPERTS)
        shifts = jax.random.randint(subkeys[1], (EXPERTS // 2,), 0, headroom + 1).at[0].set(headroom)
        halves = jnp.concatenate([mean_load + shifts, mean_load - shifts]).astype(jnp.int32)
        load_count = jnp.zeros((EXPERTS,), jnp.int32).at[pairing].set(halves)
        run_end = jnp.cumsum(load_count)
        starts = run_end - load_count
        position = jnp.arange(pick_count, dtype=jnp.int32)
        labels = jnp.sum((position[:, None] >= run_end[None, :]).astype(jnp.int32), axis=1)
        priority = jax.random.permutation(subkeys[2], pick_count).astype(jnp.int32)
        sorting = jnp.argsort(labels * pick_count + priority, stable=True)
        ranking = jnp.zeros((pick_count,), jnp.int32).at[sorting].set(position)
        slot_of = ranking - starts[labels]
        token_perm = jax.random.permutation(subkeys[3], GROUP).astype(jnp.int32)
        swapped = jax.random.randint(subkeys[4], (GROUP,), 0, 2).astype(jnp.int32)
        first_pos = token_perm + swapped * GROUP
        second_pos = token_perm + (1 - swapped) * GROUP
        route_pairs = jnp.stack([labels[first_pos], labels[second_pos]], axis=1)
        slot_pairs = jnp.stack([slot_of[first_pos], slot_of[second_pos]], axis=1)
        return (route_pairs, slot_pairs)
    all_routes, all_slots = jax.vmap(one_group)(jax.random.split(base_key, groups))
    return (all_routes.reshape(TOKENS, 2).astype(jnp.int32), all_slots.reshape(TOKENS, 2).astype(jnp.int32))


def draw_expert_routes(key, part):
    return route_table(key)[0]


def draw_expert_slots(key, part):
    return route_table(key)[1]


def draw_seq_lengths(key, part):
    own_key = jax.random.fold_in(key, 7)
    first_key, second_key = jax.random.split(own_key)
    drawn = jax.random.randint(first_key, (SEQS,), LEN // 4, LEN + 1)
    chosen = jax.random.randint(second_key, (), 0, SEQS)
    return drawn.at[chosen].set(LEN).astype(jnp.int32)


def levels(stream_key, shape, pieces, low, largest):
    def one(dim, parts):
        heights = jax.random.uniform(jax.random.fold_in(jax.random.fold_in(stream_key, 6), dim), (parts,), jnp.float32, low / len(pieces), largest / len(pieces))
        return jnp.repeat(jnp.exp(heights), shape[dim] // parts).reshape((-1,) + (1,) * (len(shape) - dim - 1))

    level = one(*pieces[0])
    for cut in pieces[1:]:
        level = level * one(*cut)
    return level


def gaussian(stream_key, dims, spread, reach, cuts=(), kind=jnp.bfloat16):
    loudness = levels(stream_key, dims, cuts, -0.22, 0.18) if cuts else 1.0
    entries = jax.random.normal(stream_key, dims, jnp.float32) * spread * loudness
    return jnp.minimum(jnp.maximum(entries, -reach), reach).astype(kind)


def setup_inputs(seed: int = 0) -> dict:
    arg_keys = jax.random.split(jax.random.key(seed), 19)
    return {
        "tokens": gaussian(arg_keys[0], (TOKENS, D), 1.0, 6.0, ((0, 32),)),
        "cotangent": gaussian(arg_keys[1], (TOKENS, D), 1.0, 6.0, ((0, 32),)),
        "seq_lengths": draw_seq_lengths(jax.random.fold_in(arg_keys[18], 71), 0),
        "expert_routes": draw_expert_routes(jax.random.fold_in(arg_keys[18], 71), 0),
        "expert_slots": draw_expert_slots(jax.random.fold_in(arg_keys[18], 71), 0),
        "attn_gain": jnp.clip(1.0 + 0.1 * jax.random.normal(arg_keys[5], (D,), jnp.float32), 0.5, 1.5).astype(jnp.bfloat16),
        "ffn_gain": jnp.clip(1.0 + 0.1 * jax.random.normal(arg_keys[6], (D,), jnp.float32), 0.5, 1.5).astype(jnp.bfloat16),
        "router_weight": gaussian(arg_keys[7], (D, EXPERTS), (2 * D) ** -0.5, 0.15625, ((0, 32),)),
        "query_weight": gaussian(arg_keys[8], (D, ATT), D ** -0.5, 0.21875, ((0, 8), (1, 4))),
        "key_weight": gaussian(arg_keys[9], (D, ATT), D ** -0.5, 0.21875, ((0, 8), (1, 4))),
        "value_weight": gaussian(arg_keys[10], (D, ATT), D ** -0.5, 0.21875, ((0, 8), (1, 4))),
        "out_weight": gaussian(arg_keys[11], (ATT, D), (D // 32) ** -0.5, 1.25, ((0, 4), (1, 8))),
        "shared_gate": gaussian(arg_keys[12], (D, FFS), D ** -0.5, 0.21875, ((0, 8), (1, 4))),
        "shared_up": gaussian(arg_keys[13], (D, FFS), D ** -0.5, 0.21875, ((0, 8), (1, 4))),
        "shared_down": gaussian(arg_keys[14], (FFS, D), FFS ** -0.5, 0.125, ((0, 4), (1, 8))),
        "expert_gate": gaussian(arg_keys[15], (EXPERTS, D, FF), D ** -0.5, 0.21875, ((1, 8), (2, 4))),
        "expert_up": gaussian(arg_keys[16], (EXPERTS, D, FF), D ** -0.5, 0.21875, ((1, 8), (2, 4))),
        "expert_down": gaussian(arg_keys[17], (EXPERTS, FF, D), FF ** -0.5, 0.125, ((1, 4), (2, 8))),
    }


EPSILON = 1e-06
MASKED_SCORE = -1e+30
PRECISE = lax.Precision.HIGHEST

@jax.custom_vjp
def low(v):
    return lax.optimization_barrier(v.astype(jnp.bfloat16)).astype(jnp.float32)

@jax.custom_vjp
def low_back(v):
    return v

def low_keep(v):
    return (low(v), None)

def low_pass(kept, grad):
    return (grad,)

def back_keep(v):
    return (v, None)

def back_low(kept, grad):
    return (low(grad),)
low.defvjp(low_keep, low_pass)
low_back.defvjp(back_keep, back_low)

def both_round(value):
    return low_back(low(value))

def mat_prod(left_mat, right_mat):
    return jnp.dot(left_mat, right_mat, precision=PRECISE, preferred_element_type=jnp.float32)

def rms_norm(rows_in, gain_row):
    inverse = lax.rsqrt(lax.optimization_barrier(jnp.mean(rows_in * rows_in, axis=-1, keepdims=True)) + EPSILON)
    return rows_in * inverse * gain_row

def swiglu(gate_value, up_value):
    return jax.nn.silu(gate_value) * up_value

def layer_group(weights, rows_in, lengths, routes, slot_ids):
    attn_gain, ffn_gain, router_weight, query_weight, key_weight, value_weight, out_weight, shared_gate, shared_up, shared_down, expert_gate, expert_up, expert_down = weights
    normed_attn = low(rms_norm(rows_in, attn_gain))
    query_all = both_round(mat_prod(normed_attn, query_weight)).reshape(SEQ_GRP, LEN, HEADS, HD)
    key_all = both_round(mat_prod(normed_attn, key_weight)).reshape(SEQ_GRP, LEN, HEADS, HD)
    value_all = both_round(mat_prod(normed_attn, value_weight)).reshape(SEQ_GRP, LEN, HEADS, HD)
    scores = low_back(jnp.einsum('sqhd,skhd->shqk', query_all, key_all, precision=PRECISE) * HD ** (-0.5))
    position = jnp.arange(LEN)
    allowed = (position[None, None, None, :] <= position[None, None, :, None]) & (position[None, None, None, :] < lengths[:, None, None, None])
    scores = jnp.where(allowed, scores, MASKED_SCORE)
    row_max = lax.optimization_barrier(jnp.max(scores, axis=-1, keepdims=True))
    exp_scores = jnp.exp(scores - row_max)
    attn_probs = exp_scores / lax.optimization_barrier(jnp.sum(exp_scores, axis=-1, keepdims=True))
    attended = both_round(jnp.einsum('shqk,skhd->sqhd', low(attn_probs), value_all, precision=PRECISE)).reshape(GROUP, HEADS * HD)
    residual = rows_in + low_back(mat_prod(attended, out_weight))
    normed_ffn = low(rms_norm(residual, ffn_gain))
    logits = mat_prod(normed_ffn, router_weight)
    first_logit = jnp.take_along_axis(logits, routes[:, 0:1], axis=1)[:, 0]
    second = jnp.take_along_axis(logits, routes[:, 1:2], axis=1)[:, 0]
    gate_first = jax.nn.sigmoid(first_logit - second)
    gate_second = jax.nn.sigmoid(second - first_logit)
    flat_slot = routes * CAP + slot_ids
    dispatched = jnp.zeros((EXPERTS * CAP, D), jnp.float32)
    dispatched = dispatched.at[flat_slot[:, 0]].add(normed_ffn).at[flat_slot[:, 1]].add(normed_ffn)
    dispatched = dispatched.reshape(EXPERTS, CAP, D)
    gate_part = low_back(jnp.einsum('ecd,edf->ecf', dispatched, expert_gate, precision=PRECISE))
    up_part = low_back(jnp.einsum('ecd,edf->ecf', dispatched, expert_up, precision=PRECISE))
    hidden = low(swiglu(gate_part, up_part))
    expert_out = low_back(jnp.einsum('ecf,efd->ecd', hidden, expert_down, precision=PRECISE)).reshape(EXPERTS * CAP, D)
    mixture = gate_first[:, None] * expert_out[flat_slot[:, 0]] + gate_second[:, None] * expert_out[flat_slot[:, 1]]
    shared_gate_part = low_back(mat_prod(normed_ffn, shared_gate))
    shared_up_part = low_back(mat_prod(normed_ffn, shared_up))
    shared_out = mat_prod(low(swiglu(shared_gate_part, shared_up_part)), shared_down)
    branch = low_back(mixture + shared_out)
    token_pos = jnp.arange(GROUP) % LEN
    which_seq = jnp.arange(GROUP) // LEN
    live_rows = (token_pos < lengths[which_seq]).astype(jnp.float32)
    return live_rows[:, None] * (residual + branch)

def reference(tokens, cotangent, seq_lengths, expert_routes, expert_slots, attn_gain, ffn_gain, router_weight, query_weight, key_weight, value_weight, out_weight, shared_gate, shared_up, shared_down, expert_gate, expert_up, expert_down):
    weights = tuple((weight_item.astype(jnp.float32) for weight_item in (attn_gain, ffn_gain, router_weight, query_weight, key_weight, value_weight, out_weight, shared_gate, shared_up, shared_down, expert_gate, expert_up, expert_down)))
    groups = TOKENS // GROUP
    lengths_all = seq_lengths.reshape(groups, SEQ_GRP)
    routes_all = expert_routes.reshape(groups, GROUP, 2)
    slots_all = expert_slots.reshape(groups, GROUP, 2)

    def forward(rows_all, weight_set):
        blocks = rows_all.reshape(groups, GROUP, D)
        group_step = jax.checkpoint(layer_group)
        result = lax.map(lambda block_item: group_step(weight_set, block_item[0], block_item[1], block_item[2], block_item[3]), (blocks, lengths_all, routes_all, slots_all))
        return result.reshape(TOKENS, D)
    output, pull_back = jax.vjp(forward, tokens.astype(jnp.float32), weights)
    d_tokens, d_weights = pull_back(cotangent.astype(jnp.float32))
    return (output.astype(jnp.bfloat16), d_tokens, d_weights[0], d_weights[1], d_weights[2], d_weights[3], d_weights[4], d_weights[5], d_weights[6], d_weights[7], d_weights[8], d_weights[9], d_weights[10], d_weights[11], d_weights[12])
```

```python
import functools

import jax
import jax.numpy as jnp
from jax import lax
from jax.experimental import pallas as pl
from jax.experimental.pallas import tpu as pltpu
from jax.sharding import PartitionSpec as P

HD = 64
EXPERTS = 8
LEN = 1024
CAP = 320
EPSILON = 1e-06
MASKED_SCORE = -1e30
BF = jnp.bfloat16
F32 = jnp.float32
PACK = 128


def dot_float(left_mat, right_mat):
    return jnp.dot(left_mat, right_mat, preferred_element_type=F32)


def dot_left_t(left_mat, right_mat):
    return lax.dot_general(left_mat, right_mat, (((0,), (0,)), ((), ())), preferred_element_type=F32)


def dot_right_t(left_mat, right_mat):
    return lax.dot_general(left_mat, right_mat, (((1,), (1,)), ((), ())), preferred_element_type=F32)


def norm_apply(rows_in, gain_row):
    inverse = lax.rsqrt(jnp.mean(rows_in * rows_in, axis=-1, keepdims=True) + EPSILON)
    return (rows_in * inverse * gain_row, inverse)


def norm_back(rows_in, inverse, gain_row, upstream):
    scaled = upstream * gain_row
    gain_grad = jnp.sum(upstream * rows_in * inverse, axis=0)
    rows_grad = inverse * scaled - rows_in * inverse**3 * jnp.mean(
        scaled * rows_in, axis=-1, keepdims=True
    )
    return (rows_grad, gain_grad)


def split_heads(matrix, seq_count, head_size):
    row_total = matrix.shape[0]
    head_count = matrix.shape[1] // head_size
    shaped = matrix.reshape(seq_count, row_total // seq_count, head_count, head_size)
    return shaped.transpose(0, 2, 1, 3).reshape(
        seq_count * head_count, row_total // seq_count, head_size
    )


def merge_heads(matrix, seq_count):
    item_count, seq_len, head_size = matrix.shape
    head_count = item_count // seq_count
    shaped = matrix.reshape(seq_count, head_count, seq_len, head_size)
    return shaped.transpose(0, 2, 1, 3).reshape(seq_count * seq_len, head_count * head_size)


def masked_scores(query_rows, key_rows, length):
    seq_len = query_rows.shape[0]
    scores = dot_right_t(query_rows, key_rows) * query_rows.shape[1] ** (-0.5)
    row_pos = lax.broadcasted_iota(jnp.int32, (seq_len, seq_len), 0)
    col_pos = lax.broadcasted_iota(jnp.int32, (seq_len, seq_len), 1)
    allowed = (col_pos <= row_pos) & (col_pos < length)
    return jnp.where(allowed, scores, MASKED_SCORE)


def attend_forward(item_parts):
    query_rows, key_rows, value_rows, length = item_parts
    scores = masked_scores(query_rows, key_rows, length)
    row_max = jnp.max(scores, axis=-1, keepdims=True)
    exp_scores = jnp.exp(scores - row_max)
    row_total = jnp.sum(exp_scores, axis=-1, keepdims=True)
    attn_probs = exp_scores / row_total
    attended = dot_float(attn_probs.astype(BF), value_rows).astype(BF)
    return (attended, (row_max + jnp.log(row_total))[:, 0])


def attend_back(item_parts):
    query_rows, key_rows, value_rows, length, grad_rows, log_total = item_parts
    scores = masked_scores(query_rows, key_rows, length)
    attn_probs = jnp.exp(scores - log_total[:, None])
    grad_probs = dot_right_t(grad_rows, value_rows)
    inner_sum = jnp.sum(attn_probs * grad_probs, axis=-1, keepdims=True)
    grad_scores = (attn_probs * (grad_probs - inner_sum)).astype(BF)
    factor = query_rows.shape[1] ** (-0.5)
    grad_query = (dot_float(grad_scores, key_rows) * factor).astype(BF)
    grad_key = (dot_left_t(grad_scores, query_rows) * factor).astype(BF)
    grad_value = dot_left_t(attn_probs.astype(BF), grad_rows).astype(BF)
    return (grad_query, grad_key, grad_value)


def place_body(count, rows, pos_ref, *refs):
    out_ref = refs[count]
    for j in range(count):
        start = pl.multiple_of(pos_ref[j] * rows, rows)
        out_ref[pl.ds(start, rows), :] = refs[j][...]


def place(pieces, positions):
    count = len(pieces)
    if count == 1:
        return pieces[0]
    rows, cols = pieces[0].shape
    return pl.pallas_call(
        functools.partial(place_body, count, rows),
        out_shape=jax.ShapeDtypeStruct((rows * count, cols), pieces[0].dtype),
        in_specs=[pl.BlockSpec(memory_space=pltpu.SMEM)] + [pl.BlockSpec()] * count,
        out_specs=pl.BlockSpec(),
        name="place",
    )(positions, *pieces)


def moe_body(tp, np, rows, pos_ref, idx_ref, col_ref, router_ref, *refs):
    ffn_refs = refs[:tp]
    grad_refs = refs[tp : 2 * tp]
    refs = refs[2 * tp :]
    wa_refs = refs[:np]
    wb_refs = refs[np : 2 * np]
    refs = refs[2 * np :]
    branch_refs = refs[:tp]
    dffn_refs = refs[tp : 2 * tp]
    drouter_ref = refs[2 * tp]
    refs = refs[2 * tp + 1 :]
    da_refs = refs[:np]
    db_refs = refs[np : 2 * np]
    xg, w_scr, dw_scr, y_scr, gate_scr, gg_scr, glt_scr, act_scr = refs[2 * np :]
    step = pl.program_id(0)
    own = ffn_refs[0].shape[0]
    width = ffn_refs[0].shape[1]
    group = own * tp
    half = wa_refs[0].shape[-1]
    ff = 2 * half
    slots = EXPERTS * CAP

    @pl.when(step == 0)
    def _():
        for s in range(tp):
            start = pl.multiple_of(pos_ref[s] * own, own)
            xg[pl.ds(start, own), :width] = ffn_refs[s][...]
            xg[pl.ds(start, own), width:] = grad_refs[s][...]
        logits = dot_right_t(router_ref[...], xg[:, :width])[:EXPERTS]
        ids = lax.broadcasted_iota(jnp.int32, (EXPERTS, group), 0)
        gap = jnp.sum(
            jnp.where(idx_ref[2:3, :] == ids, logits, 0.0)
            - jnp.where(idx_ref[3:4, :] == ids, logits, 0.0),
            axis=0,
            keepdims=True,
        )
        gate_scr[0:1, :] = jax.nn.sigmoid(gap)
        gate_scr[1:2, :] = jax.nn.sigmoid(-gap)
        gg_scr[...] = jnp.zeros_like(gg_scr)

    for m in range(3):
        for j in range(np):
            start = pl.multiple_of(pos_ref[tp + j] * rows, rows)
            w_scr[m, pl.ds(start, rows), :half] = wa_refs[j][m]
            w_scr[m, pl.ds(start, rows), half:] = wb_refs[j][m]

    def store_grads():
        for m in range(3):
            for j in range(np):
                start = pl.multiple_of(pos_ref[tp + j] * rows, rows)
                da_refs[j][m] = dw_scr[m, pl.ds(start, rows), :half].astype(BF)
                db_refs[j][m] = dw_scr[m, pl.ds(start, rows), half:].astype(BF)

    @pl.when(step < EXPERTS)
    def _():
        ids = lax.broadcasted_iota(jnp.int32, (CAP, group), 0) + step * CAP
        first = idx_ref[0:1, :] == ids
        second = idx_ref[1:2, :] == ids
        pick = jnp.where(first | second, 1.0, 0.0).astype(BF)
        slot_gate = jnp.sum(
            jnp.where(first, gate_scr[0:1, :], jnp.where(second, gate_scr[1:2, :], 0.0)),
            axis=1,
            keepdims=True,
        )
        disp = dot_float(pick, xg[:, :width]).astype(BF)
        grad_rows = dot_float(pick, xg[:, width:])
        gate_part = dot_float(disp, w_scr[0])
        up_part = dot_float(disp, w_scr[1])
        sig = jax.nn.sigmoid(gate_part)
        act = gate_part * sig
        hidden = (act * up_part).astype(BF)
        rows_out = dot_right_t(hidden, w_scr[2])
        slot_grad = jnp.sum(grad_rows * rows_out, axis=1, keepdims=True)
        gg_scr[0:1, :] += jnp.sum(jnp.where(first, slot_grad, 0.0), axis=0, keepdims=True)
        gg_scr[1:2, :] += jnp.sum(jnp.where(second, slot_grad, 0.0), axis=0, keepdims=True)
        grad_exp = (slot_gate * grad_rows).astype(BF)
        grad_hid = dot_float(grad_exp, w_scr[2])
        d_gate = (grad_hid * up_part * sig * (1.0 + gate_part * (1.0 - sig))).astype(BF)
        d_up = (grad_hid * act).astype(BF)
        grad_disp = dot_right_t(d_gate, w_scr[0]) + dot_right_t(d_up, w_scr[1])
        base = pl.multiple_of(step * CAP, CAP)
        y_scr[pl.ds(base, CAP), :width] = (slot_gate * rows_out).astype(BF)
        y_scr[pl.ds(base, CAP), width:] = grad_disp.astype(BF)
        dw_scr[0] = dot_left_t(disp, d_gate)
        dw_scr[1] = dot_left_t(disp, d_up)
        dw_scr[2] = dot_left_t(grad_exp, hidden)
        store_grads()

    @pl.when(step == EXPERTS)
    def _():
        ids = lax.broadcasted_iota(jnp.int32, (EXPERTS, group), 0)
        change = (gg_scr[0:1, :] - gg_scr[1:2, :]) * gate_scr[0:1, :] * gate_scr[1:2, :]
        grad_logits = jnp.where(idx_ref[2:3, :] == ids, change, 0.0) - jnp.where(
            idx_ref[3:4, :] == ids, change, 0.0
        )
        high = grad_logits.astype(BF)
        low = (grad_logits - high.astype(F32)).astype(BF)
        both = jnp.concatenate([high, low], axis=0)
        router_grads = dot_float(both, xg[:, :width])
        drouter_ref[...] = router_grads[:EXPERTS] + router_grads[EXPERTS:]
        padded = jnp.concatenate(
            [grad_logits, jnp.zeros((128 - EXPERTS, group), F32)], axis=0
        )
        glt_scr[...] = padded.T.astype(BF)
        for s in range(tp):
            start = pl.multiple_of(pos_ref[s] * own, own)
            rows_x = xg[pl.ds(start, own), :width]
            rows_g = xg[pl.ds(start, own), width:]
            gate_part = dot_float(rows_x, w_scr[0])
            up_part = dot_float(rows_x, w_scr[1])
            sig = jax.nn.sigmoid(gate_part)
            act = gate_part * sig
            hidden = (act * up_part).astype(BF)
            grad_hid = dot_float(rows_g, w_scr[2])
            d_gate = (grad_hid * up_part * sig * (1.0 + gate_part * (1.0 - sig))).astype(BF)
            d_up = (grad_hid * act).astype(BF)
            act_scr[pl.ds(start, own), :ff] = d_gate
            act_scr[pl.ds(start, own), ff : 2 * ff] = d_up
            act_scr[pl.ds(start, own), 2 * ff :] = hidden
            cols = col_ref[pl.ds(start, own), :]
            slot_ids = lax.broadcasted_iota(jnp.int32, (own, slots), 1)
            pick = jnp.where(
                (cols[:, 0:1] == slot_ids) | (cols[:, 1:2] == slot_ids), 1.0, 0.0
            ).astype(BF)
            branch_refs[s][...] = (
                dot_right_t(hidden, w_scr[2]) + dot_float(pick, y_scr[:, :width])
            ).astype(BF)
            routed = dot_float(glt_scr[pl.ds(start, own), :], router_ref[...])
            dffn_refs[s][...] = (
                dot_right_t(d_gate, w_scr[0])
                + dot_right_t(d_up, w_scr[1])
                + dot_float(pick, y_scr[:, width:])
                + routed
            ).astype(BF)
        dw_scr[0] = dot_left_t(xg[:, :width], act_scr[:, :ff])
        dw_scr[1] = dot_left_t(xg[:, :width], act_scr[:, ff : 2 * ff])
        dw_scr[2] = dot_left_t(xg[:, width:], act_scr[:, 2 * ff :])
        store_grads()


def moe(tp, positions, idx_rows, idx_cols, router_rows, ffn, grads, wa, wb):
    np = len(wa)
    own, width = ffn[0].shape
    group = own * tp
    mats, _, rows, half = wa[0].shape
    whole = pl.BlockSpec(index_map=lambda e, p: (0, 0))
    full = lambda a: pl.BlockSpec(a.shape, lambda e, p: (0, 0))
    piece = pl.BlockSpec((None, 3, rows, half), lambda e, p: (e, 0, 0, 0))
    tok = pl.BlockSpec((own, width), lambda e, p: (0, 0))
    out_shape = (
        [jax.ShapeDtypeStruct((own, width), BF)] * (2 * tp)
        + [jax.ShapeDtypeStruct((EXPERTS, width), F32)]
        + [jax.ShapeDtypeStruct(wa[0].shape, BF)] * (2 * np)
    )
    outs = pl.pallas_call(
        functools.partial(moe_body, tp, np, rows),
        out_shape=out_shape,
        grid_spec=pltpu.PrefetchScalarGridSpec(
            num_scalar_prefetch=1,
            grid=(EXPERTS + 1,),
            in_specs=[full(idx_rows), full(idx_cols), full(router_rows)]
            + [tok] * (2 * tp)
            + [piece] * (2 * np),
            out_specs=[tok] * (2 * tp)
            + [pl.BlockSpec((EXPERTS, width), lambda e, p: (0, 0))]
            + [piece] * (2 * np),
            scratch_shapes=[
                pltpu.VMEM((group, 2 * width), BF),
                pltpu.VMEM((3, width, 2 * half), BF),
                pltpu.VMEM((3, width, 2 * half), F32),
                pltpu.VMEM((EXPERTS * CAP, 2 * width), BF),
                pltpu.VMEM((8, group), F32),
                pltpu.VMEM((8, group), F32),
                pltpu.VMEM((group, 128), BF),
                pltpu.VMEM((group, 6 * half), BF),
            ],
        ),
        compiler_params=pltpu.CompilerParams(
            dimension_semantics=("arbitrary",), vmem_limit_bytes=60 * 1024 * 1024
        ),
        name="moe",
    )(positions, idx_rows, idx_cols, router_rows, *ffn, *grads, *wa, *wb)
    return (
        outs[:tp],
        outs[tp : 2 * tp],
        outs[2 * tp],
        outs[2 * tp + 1 : 2 * tp + 1 + np],
        outs[2 * tp + 1 + np :],
    )


def shards(
    n,
    tp,
    tokens,
    cotangent,
    seq_lengths,
    expert_routes,
    expert_slots,
    attn_gain,
    ffn_gain,
    router_weight,
    query_weight,
    key_weight,
    value_weight,
    out_weight,
    shared_gate,
    shared_up,
    shared_down,
    expert_gate,
    expert_up,
    expert_down,
):
    own_rows, width = tokens.shape
    t_own = lax.axis_index("tp")
    f_own = lax.axis_index("fsdp")
    piece_rows = query_weight.shape[0]
    cube = n & (n - 1) == 0 and 4 <= n <= 8 and piece_rows % 16 == 0
    bits = [1 << b for b in range(n.bit_length() - 1)]
    order_a = bits[1:] + bits[:1]
    order_b = bits[1:][::-1] + bits[:1]

    def shift(value, s):
        return lax.ppermute(value, "tp", [(i, (i + s) % tp) for i in range(tp)])

    def flip(value, k):
        return lax.ppermute(value, "fsdp", [(i, i ^ k) for i in range(n)])

    def tp_gather(value):
        return [value] + [shift(value, tp - s) for s in range(1, tp)]

    def tp_scatter(pieces):
        total = pieces[0].astype(F32)
        for s in range(1, tp):
            total = total + shift(pieces[s], s).astype(F32)
        return total

    def fs_gather(value, order, axis):
        if not cube:
            return [lax.all_gather(value, "fsdp", axis=axis, tiled=True)]
        held = {0: value}
        for k in order:
            held.update({i | k: flip(held[i], k) for i in list(held)})
        return [held[i] for i in range(n)]

    def fs_scatter(pieces, order, axis):
        if not cube:
            return lax.psum_scatter(
                pieces[0], "fsdp", scatter_dimension=axis, tiled=True
            ).astype(F32)
        held = dict(enumerate(pieces))
        for k in order[::-1]:
            low = [i for i in held if not i & k]
            last = len(low) == 1
            got = {i: flip(held[i | k], k) for i in low}
            held = {i: held[i].astype(F32) + got[i].astype(F32) for i in low}
            if not last:
                held = {i: v.astype(BF) for i, v in held.items()}
        return held[0]

    tp_pos = (t_own + jnp.arange(tp, dtype=jnp.int32)) % tp
    if cube:
        fs_pos = f_own ^ jnp.arange(n, dtype=jnp.int32)
    else:
        fs_pos = jnp.zeros((1,), jnp.int32)

    token_pieces = tp_gather(tokens)
    packed_gains = jnp.concatenate(
        [
            router_weight,
            attn_gain[:, None],
            ffn_gain[:, None],
            jnp.zeros((attn_gain.shape[0], PACK - EXPERTS - 2), BF),
        ],
        axis=1,
    )
    gain_pieces = tp_gather(packed_gains)
    gain_rows = jnp.concatenate(gain_pieces + gain_pieces[:-1], axis=0)
    gain_rows = lax.dynamic_slice_in_dim(
        gain_rows, ((tp - t_own) % tp) * attn_gain.shape[0], piece_rows, 0
    )
    att_cols = query_weight.shape[1]
    attn_pack = jnp.concatenate(
        [query_weight, key_weight, value_weight, out_weight.T, gain_rows], axis=1
    )
    attn_full = place(fs_gather(attn_pack, order_a, 0), fs_pos)

    stacked = jnp.stack(
        [
            jnp.concatenate([expert_gate, shared_gate[None]], axis=0),
            jnp.concatenate([expert_up, shared_up[None]], axis=0),
            jnp.concatenate([expert_down, shared_down[None]], axis=0).transpose(0, 2, 1),
        ],
        axis=1,
    )
    half = stacked.shape[-1] // 2
    weights_a = fs_gather(stacked[..., :half], order_a, 2)
    weights_b = fs_gather(stacked[..., half:], order_b, 2)

    offset = t_own * own_rows
    row_place = offset + lax.iota(jnp.int32, own_rows)
    seq_count = seq_lengths.shape[0]
    seq_ids = lax.iota(jnp.int32, seq_count)
    row_length = jnp.sum(
        jnp.where((row_place // LEN)[:, None] == seq_ids[None, :], seq_lengths[None, :], 0), axis=1
    )
    live_rows = (row_place % LEN < row_length).astype(F32)[:, None]
    grad_out = live_rows * cotangent.astype(F32)
    grad_pieces = tp_gather(grad_out.astype(BF))

    query_full = attn_full[:, :att_cols]
    key_full = attn_full[:, att_cols : 2 * att_cols]
    value_full = attn_full[:, 2 * att_cols : 3 * att_cols]
    out_full = attn_full[:, 3 * att_cols : 4 * att_cols]
    small = attn_full[:, 4 * att_cols : 4 * att_cols + 16].T
    gain_attn = small[EXPERTS].astype(F32)
    gain_ffn = small[EXPERTS + 1].astype(F32)
    router_rows = jnp.concatenate(
        [small[:EXPERTS], jnp.zeros((128 - EXPERTS, width), BF)], axis=0
    )

    token_rows = place(token_pieces, tp_pos)
    attn_rows = norm_apply(token_rows.astype(F32), gain_attn)[0].astype(BF)
    query_items = split_heads(dot_float(attn_rows, query_full).astype(BF), seq_count, HD)
    key_items = split_heads(dot_float(attn_rows, key_full).astype(BF), seq_count, HD)
    value_items = split_heads(dot_float(attn_rows, value_full).astype(BF), seq_count, HD)
    item_lengths = jnp.repeat(seq_lengths, query_items.shape[0] // seq_count)
    attended_items, log_totals = lax.map(
        attend_forward, (query_items, key_items, value_items, item_lengths)
    )
    attended = merge_heads(attended_items, seq_count)
    attn_part = dot_right_t(attended, out_full).astype(BF)

    def cut(value, positions, rows):
        return [
            lax.dynamic_slice_in_dim(value, positions[j] * rows, rows, 0)
            for j in range(positions.shape[0])
        ]

    rows_in = tokens.astype(F32)
    residual = rows_in + tp_scatter(cut(attn_part, tp_pos, own_rows))
    normed_ffn, inverse_ffn = norm_apply(residual, gain_ffn)
    ffn_pieces = tp_gather(normed_ffn.astype(BF))

    flat = expert_routes * CAP + expert_slots
    idx_rows = jnp.concatenate(
        [flat.T, expert_routes.T, jnp.zeros((4, flat.shape[0]), jnp.int32)], axis=0
    )
    branch_pieces, dffn_pieces, router_grad, grads_a, grads_b = moe(
        tp,
        jnp.concatenate([tp_pos, fs_pos]),
        idx_rows,
        flat,
        router_rows,
        ffn_pieces,
        grad_pieces,
        weights_a,
        weights_b,
    )
    grad_ffn_own = tp_scatter(dffn_pieces)
    grad_residual_norm, ffn_gain_grad = norm_back(residual, inverse_ffn, gain_ffn, grad_ffn_own)
    grad_residual = grad_out + grad_residual_norm
    grad_attn_rows = place(tp_gather(grad_residual.astype(BF)), tp_pos)
    out_grad = dot_left_t(grad_attn_rows, attended)
    grad_attended = dot_float(grad_attn_rows, out_full).astype(BF)
    grad_items = split_heads(grad_attended, seq_count, HD)
    grad_query_items, grad_key_items, grad_value_items = lax.map(
        attend_back, (query_items, key_items, value_items, item_lengths, grad_items, log_totals)
    )
    grad_query = merge_heads(grad_query_items, seq_count)
    grad_key = merge_heads(grad_key_items, seq_count)
    grad_value = merge_heads(grad_value_items, seq_count)
    grad_normed = (
        dot_right_t(grad_query, query_full)
        + dot_right_t(grad_key, key_full)
        + dot_right_t(grad_value, value_full)
    )
    grad_attn_own = tp_scatter(cut(grad_normed.astype(BF), tp_pos, own_rows))
    inverse_attn = lax.rsqrt(jnp.mean(rows_in * rows_in, axis=-1, keepdims=True) + EPSILON)
    grad_rows_norm, attn_gain_grad = norm_back(rows_in, inverse_attn, gain_attn, grad_attn_own)
    grad_tokens = grad_residual + grad_rows_norm
    layer_out = (live_rows * (residual + tp_scatter(branch_pieces))).astype(BF)

    small_grads = jnp.concatenate(
        [
            router_grad,
            attn_gain_grad[None],
            ffn_gain_grad[None],
            jnp.zeros((PACK - EXPERTS - 2, width), F32),
        ],
        axis=0,
    ).T
    pack_grads = jnp.concatenate(
        [
            dot_left_t(attn_rows, grad_query),
            dot_left_t(attn_rows, grad_key),
            dot_left_t(attn_rows, grad_value),
            out_grad,
            small_grads,
        ],
        axis=1,
    ).astype(BF)
    if cube:
        pack_pieces = cut(pack_grads, fs_pos, piece_rows)
    else:
        pack_pieces = [pack_grads]
    pack_own = fs_scatter(pack_pieces, order_a, 0)
    small_own = tp_scatter(
        cut(pack_own[:, 4 * att_cols : 4 * att_cols + 16], tp_pos, attn_gain.shape[0])
    )
    own_grads = jnp.concatenate(
        [fs_scatter(grads_a, order_a, 2), fs_scatter(grads_b, order_b, 2)], axis=-1
    )
    return (
        layer_out,
        grad_tokens,
        small_own[:, EXPERTS],
        small_own[:, EXPERTS + 1],
        small_own[:, :EXPERTS],
        pack_own[:, :att_cols],
        pack_own[:, att_cols : 2 * att_cols],
        pack_own[:, 2 * att_cols : 3 * att_cols],
        pack_own[:, 3 * att_cols : 4 * att_cols].T,
        own_grads[EXPERTS, 0],
        own_grads[EXPERTS, 1],
        own_grads[EXPERTS, 2].T,
        own_grads[:EXPERTS, 0],
        own_grads[:EXPERTS, 1],
        own_grads[:EXPERTS, 2].transpose(0, 2, 1),
    )


def solution(mesh):
    placed = (
        P(("fsdp", "tp"), None),
        P(("fsdp", "tp"), None),
        P("fsdp"),
        P("fsdp", None),
        P("fsdp", None),
        P(("fsdp", "tp")),
        P(("fsdp", "tp")),
        P(("fsdp", "tp"), None),
        P("fsdp", "tp"),
        P("fsdp", "tp"),
        P("fsdp", "tp"),
        P("tp", "fsdp"),
        P("fsdp", "tp"),
        P("fsdp", "tp"),
        P("tp", "fsdp"),
        P(None, "fsdp", "tp"),
        P(None, "fsdp", "tp"),
        P(None, "tp", "fsdp"),
    )
    return jax.shard_map(
        functools.partial(shards, mesh.shape["fsdp"], mesh.shape["tp"]),
        mesh=mesh,
        in_specs=placed,
        out_specs=(
            P(("fsdp", "tp"), None),
            P(("fsdp", "tp"), None),
            P(("fsdp", "tp")),
            P(("fsdp", "tp")),
            P(("fsdp", "tp"), None),
            P("fsdp", "tp"),
            P("fsdp", "tp"),
            P("fsdp", "tp"),
            P("tp", "fsdp"),
            P("fsdp", "tp"),
            P("fsdp", "tp"),
            P("tp", "fsdp"),
            P(None, "fsdp", "tp"),
            P(None, "fsdp", "tp"),
            P(None, "tp", "fsdp"),
        ),
        check_vma=False,
    )
```

```python
import functools

import jax
import jax.numpy as jnp
from jax import lax
from jax.experimental import pallas as pl
from jax.experimental.pallas import tpu as pltpu
from jax.sharding import PartitionSpec as P

HD = 64
EXPERTS = 8
LEN = 1024
CAP = 320
EPSILON = 1e-06
MASKED_SCORE = -1e30
BF = jnp.bfloat16
F32 = jnp.float32
PACK = 128


def dot_float(left_mat, right_mat):
    return jnp.dot(left_mat, right_mat, preferred_element_type=F32)


def dot_left_t(left_mat, right_mat):
    return lax.dot_general(left_mat, right_mat, (((0,), (0,)), ((), ())), preferred_element_type=F32)


def dot_right_t(left_mat, right_mat):
    return lax.dot_general(left_mat, right_mat, (((1,), (1,)), ((), ())), preferred_element_type=F32)


def norm_apply(rows_in, gain_row):
    inverse = lax.rsqrt(jnp.mean(rows_in * rows_in, axis=-1, keepdims=True) + EPSILON)
    return (rows_in * inverse * gain_row, inverse)


def norm_back(rows_in, inverse, gain_row, upstream):
    scaled = upstream * gain_row
    gain_grad = jnp.sum(upstream * rows_in * inverse, axis=0)
    rows_grad = inverse * scaled - rows_in * inverse**3 * jnp.mean(
        scaled * rows_in, axis=-1, keepdims=True
    )
    return (rows_grad, gain_grad)


def attn_fwd_body(tp, np, pos_ref, len_ref, *refs):
    x_refs, refs = refs[:tp], refs[tp:]
    pack_refs, gain_refs, refs = refs[:np], refs[np : 2 * np], refs[2 * np :]
    part_refs, refs = refs[:tp], refs[tp:]
    rows_ref, q_ref, k_ref, v_ref, att_ref, lse_ref, w_ref, small_ref, gain_scr = refs
    own, width = x_refs[0].shape
    heads = q_ref.shape[0]
    att_width = heads * HD
    prow = pack_refs[0].shape[0]
    for j in range(np):
        start = pl.multiple_of(pos_ref[tp + j] * prow, prow)
        w_ref[pl.ds(start, prow), :] = pack_refs[j][...]
        gain_scr[pl.ds(start, prow), :] = gain_refs[j][...].astype(F32)
    small = gain_scr[...].T
    small_ref[...] = small.astype(BF)
    gain = small[EXPERTS : EXPERTS + 1, :]
    for s in range(tp):
        start = pl.multiple_of(pos_ref[s] * own, own)
        rows = norm_apply(x_refs[s][...].astype(F32), gain)[0].astype(BF)
        rows_ref[pl.ds(start, own), :] = rows
        qkv = dot_float(rows, w_ref[:, : 3 * att_width]).astype(BF)
        for h in range(heads):
            for m, ref in enumerate((q_ref, k_ref, v_ref)):
                ref[h, pl.ds(start, own), :] = qkv[:, m * att_width + h * HD :][:, :HD]
    length = len_ref[0]
    for h in range(heads):
        for i in range(tp):
            ext = (i + 1) * own
            probs, row_max, total = None, None, None
            scores = masked(q_ref[h, i * own : ext, :], k_ref[h, :ext, :], length, i * own)
            row_max = jnp.max(scores, axis=-1, keepdims=True)
            exp_scores = jnp.exp(scores - row_max)
            total = jnp.sum(exp_scores, axis=-1, keepdims=True)
            probs = (exp_scores * (1.0 / total)).astype(BF)
            att_ref[i * own : ext, h * HD : (h + 1) * HD] = dot_float(
                probs, v_ref[h, :ext, :]
            ).astype(BF)
            lse_ref[i * own : ext, h : h + 1] = row_max + jnp.log(total)
    for s in range(tp):
        start = pl.multiple_of(pos_ref[s] * own, own)
        part_refs[s][...] = dot_right_t(
            att_ref[pl.ds(start, own), :], w_ref[:, 3 * att_width :]
        ).astype(BF)


def masked(query_rows, key_rows, length, first):
    scores = dot_right_t(query_rows, key_rows) * HD ** (-0.5)
    row_pos = lax.broadcasted_iota(jnp.int32, scores.shape, 0) + first
    col_pos = lax.broadcasted_iota(jnp.int32, scores.shape, 1)
    return jnp.where((col_pos <= row_pos) & (col_pos < length), scores, MASKED_SCORE)


def attn_fwd(tp, positions, length, x_pieces, pack_pieces, gain_pieces):
    np = len(pack_pieces)
    own, width = x_pieces[0].shape
    group = own * tp
    att_width = pack_pieces[0].shape[1] // 4
    heads = att_width // HD
    shape = jax.ShapeDtypeStruct
    outs = pl.pallas_call(
        functools.partial(attn_fwd_body, tp, np),
        out_shape=[shape((own, width), BF)] * tp
        + [shape((group, width), BF)]
        + [shape((heads, group, HD), BF)] * 3
        + [
            shape((group, att_width), BF),
            shape((group, 128), F32),
            shape((width, 4 * att_width), BF),
            shape((PACK, width), BF),
        ],
        in_specs=[pl.BlockSpec(memory_space=pltpu.SMEM)] * 2
        + [pl.BlockSpec(memory_space=pltpu.VMEM)] * (tp + 2 * np),
        out_specs=[pl.BlockSpec(memory_space=pltpu.VMEM)] * (tp + 8),
        scratch_shapes=[pltpu.VMEM((width, PACK), F32)],
        compiler_params=pltpu.CompilerParams(vmem_limit_bytes=56 * 1024 * 1024),
        name="attn_fwd",
    )(positions, length, *x_pieces, *pack_pieces, *gain_pieces)
    return outs[:tp], outs[tp:]


def attn_bwd_body(tp, np, pos_ref, len_ref, *refs):
    g_refs, refs = refs[:tp], refs[tp:]
    rows_ref, q_ref, k_ref, v_ref, att_ref, lse_ref, w_ref, small_ref = refs[:8]
    refs = refs[8:]
    part_refs, refs = refs[:tp], refs[tp:]
    dpack_refs, refs = refs[:np], refs[np:]
    dgain_ref, gres, g_scr, ga_scr, dk_scr, dv_scr, dw_scr = refs
    own, width = g_refs[0].shape
    heads = q_ref.shape[0]
    att_width = heads * HD
    prow = dpack_refs[0].shape[0]
    for s in range(tp):
        start = pl.multiple_of(pos_ref[s] * own, own)
        gres[pl.ds(start, own), :] = g_refs[s][...]
    grad_att = dot_float(gres[...], w_ref[:, 3 * att_width :]).astype(BF)
    for h in range(heads):
        ga_scr[h] = grad_att[:, h * HD : (h + 1) * HD]
    dw_scr[:, 3 * att_width :] = dot_left_t(gres[...], att_ref[...])
    length = len_ref[0]
    factor = HD ** (-0.5)
    for h in range(heads):
        dk_scr[...] = jnp.zeros_like(dk_scr)
        dv_scr[...] = jnp.zeros_like(dv_scr)
        for i in range(tp):
            ext = (i + 1) * own
            q_rows = q_ref[h, i * own : ext, :]
            ga_rows = ga_scr[h, i * own : ext, :]
            scores = masked(q_rows, k_ref[h, :ext, :], length, i * own)
            probs = jnp.exp(scores - lse_ref[i * own : ext, h : h + 1])
            grad_probs = dot_right_t(ga_rows, v_ref[h, :ext, :])
            inner = jnp.sum(probs * grad_probs, axis=-1, keepdims=True)
            grad_scores = (probs * (grad_probs - inner)).astype(BF)
            g_scr[i * own : ext, h * HD : (h + 1) * HD] = (
                dot_float(grad_scores, k_ref[h, :ext, :]) * factor
            ).astype(BF)
            dk_scr[:ext, :] += dot_left_t(grad_scores, q_rows)
            dv_scr[:ext, :] += dot_left_t(probs.astype(BF), ga_rows)
        g_scr[:, att_width + h * HD : att_width + (h + 1) * HD] = (dk_scr[...] * factor).astype(BF)
        g_scr[:, 2 * att_width + h * HD : 2 * att_width + (h + 1) * HD] = dv_scr[...].astype(BF)
    dgain = jnp.zeros((1, width), F32)
    for s in range(tp):
        start = pl.multiple_of(pos_ref[s] * own, own)
        grad_rows = dot_right_t(g_scr[pl.ds(start, own), :], w_ref[:, : 3 * att_width])
        part_refs[s][...] = grad_rows.astype(BF)
        dgain = dgain + jnp.sum(
            grad_rows * rows_ref[pl.ds(start, own), :].astype(F32), axis=0, keepdims=True
        )
    dgain_ref[...] = dgain / small_ref[EXPERTS : EXPERTS + 1, :].astype(F32)
    dw_scr[:, : 3 * att_width] = dot_left_t(rows_ref[...], g_scr[...])
    for j in range(np):
        start = pl.multiple_of(pos_ref[tp + j] * prow, prow)
        dpack_refs[j][...] = dw_scr[pl.ds(start, prow), :].astype(BF)


def attn_bwd(tp, np, positions, length, g_pieces, saved):
    own, width = g_pieces[0].shape
    group = own * tp
    heads = saved[1].shape[0]
    att_width = heads * HD
    shape = jax.ShapeDtypeStruct
    outs = pl.pallas_call(
        functools.partial(attn_bwd_body, tp, np),
        out_shape=[shape((own, width), BF)] * tp
        + [shape((width // np, 4 * att_width), BF)] * np
        + [shape((1, width), F32)],
        in_specs=[pl.BlockSpec(memory_space=pltpu.SMEM)] * 2
        + [pl.BlockSpec(memory_space=pltpu.VMEM)] * (tp + 8),
        out_specs=[pl.BlockSpec(memory_space=pltpu.VMEM)] * (tp + np + 1),
        scratch_shapes=[
            pltpu.VMEM((group, width), BF),
            pltpu.VMEM((group, 3 * att_width), BF),
            pltpu.VMEM((heads, group, HD), BF),
            pltpu.VMEM((group, HD), F32),
            pltpu.VMEM((group, HD), F32),
            pltpu.VMEM((width, 4 * att_width), F32),
        ],
        compiler_params=pltpu.CompilerParams(vmem_limit_bytes=56 * 1024 * 1024),
        name="attn_bwd",
    )(positions, length, *g_pieces, *saved)
    return outs[:tp], outs[tp : tp + np], outs[tp + np]


def moe_body(tp, np, rows, pos_ref, idx_ref, col_ref, router_ref, *refs):
    ffn_refs = refs[:tp]
    grad_refs = refs[tp : 2 * tp]
    refs = refs[2 * tp :]
    wa_refs = refs[:np]
    wb_refs = refs[np : 2 * np]
    refs = refs[2 * np :]
    branch_refs = refs[:tp]
    dffn_refs = refs[tp : 2 * tp]
    drouter_ref = refs[2 * tp]
    refs = refs[2 * tp + 1 :]
    da_refs = refs[:np]
    db_refs = refs[np : 2 * np]
    xg, w_scr, dw_scr, y_scr, gate_scr, gg_scr, glt_scr, act_scr = refs[2 * np :]
    step = pl.program_id(0)
    own = ffn_refs[0].shape[0]
    width = ffn_refs[0].shape[1]
    group = own * tp
    half = wa_refs[0].shape[-1]
    ff = 2 * half
    slots = EXPERTS * CAP

    @pl.when(step == 0)
    def _():
        for s in range(tp):
            start = pl.multiple_of(pos_ref[s] * own, own)
            xg[pl.ds(start, own), :width] = ffn_refs[s][...]
            xg[pl.ds(start, own), width:] = grad_refs[s][...]
        logits = dot_right_t(router_ref[...], xg[:, :width])[:EXPERTS]
        ids = lax.broadcasted_iota(jnp.int32, (EXPERTS, group), 0)
        gap = jnp.sum(
            jnp.where(idx_ref[2:3, :] == ids, logits, 0.0)
            - jnp.where(idx_ref[3:4, :] == ids, logits, 0.0),
            axis=0,
            keepdims=True,
        )
        gate_scr[0:1, :] = jax.nn.sigmoid(gap)
        gate_scr[1:2, :] = jax.nn.sigmoid(-gap)
        gg_scr[...] = jnp.zeros_like(gg_scr)

    for m in range(3):
        for j in range(np):
            start = pl.multiple_of(pos_ref[tp + j] * rows, rows)
            w_scr[m, pl.ds(start, rows), :half] = wa_refs[j][m]
            w_scr[m, pl.ds(start, rows), half:] = wb_refs[j][m]

    def store_grads():
        for m in range(3):
            for j in range(np):
                start = pl.multiple_of(pos_ref[tp + j] * rows, rows)
                da_refs[j][m] = dw_scr[m, pl.ds(start, rows), :half].astype(BF)
                db_refs[j][m] = dw_scr[m, pl.ds(start, rows), half:].astype(BF)

    @pl.when(step < EXPERTS)
    def _():
        ids = lax.broadcasted_iota(jnp.int32, (CAP, group), 0) + step * CAP
        first = idx_ref[0:1, :] == ids
        second = idx_ref[1:2, :] == ids
        pick = jnp.where(first | second, 1.0, 0.0).astype(BF)
        slot_gate = jnp.sum(
            jnp.where(first, gate_scr[0:1, :], jnp.where(second, gate_scr[1:2, :], 0.0)),
            axis=1,
            keepdims=True,
        )
        disp = dot_float(pick, xg[:, :width]).astype(BF)
        grad_rows = dot_float(pick, xg[:, width:])
        gate_part = dot_float(disp, w_scr[0])
        up_part = dot_float(disp, w_scr[1])
        sig = jax.nn.sigmoid(gate_part)
        act = gate_part * sig
        hidden = (act * up_part).astype(BF)
        rows_out = dot_right_t(hidden, w_scr[2])
        slot_grad = jnp.sum(grad_rows * rows_out, axis=1, keepdims=True)
        gg_scr[0:1, :] += jnp.sum(jnp.where(first, slot_grad, 0.0), axis=0, keepdims=True)
        gg_scr[1:2, :] += jnp.sum(jnp.where(second, slot_grad, 0.0), axis=0, keepdims=True)
        grad_exp = (slot_gate * grad_rows).astype(BF)
        grad_hid = dot_float(grad_exp, w_scr[2])
        d_gate = (grad_hid * up_part * sig * (1.0 + gate_part * (1.0 - sig))).astype(BF)
        d_up = (grad_hid * act).astype(BF)
        grad_disp = dot_right_t(d_gate, w_scr[0]) + dot_right_t(d_up, w_scr[1])
        base = pl.multiple_of(step * CAP, CAP)
        y_scr[pl.ds(base, CAP), :width] = (slot_gate * rows_out).astype(BF)
        y_scr[pl.ds(base, CAP), width:] = grad_disp.astype(BF)
        dw_scr[0] = dot_left_t(disp, d_gate)
        dw_scr[1] = dot_left_t(disp, d_up)
        dw_scr[2] = dot_left_t(grad_exp, hidden)
        store_grads()

    @pl.when(step == EXPERTS)
    def _():
        ids = lax.broadcasted_iota(jnp.int32, (EXPERTS, group), 0)
        change = (gg_scr[0:1, :] - gg_scr[1:2, :]) * gate_scr[0:1, :] * gate_scr[1:2, :]
        grad_logits = jnp.where(idx_ref[2:3, :] == ids, change, 0.0) - jnp.where(
            idx_ref[3:4, :] == ids, change, 0.0
        )
        high = grad_logits.astype(BF)
        low = (grad_logits - high.astype(F32)).astype(BF)
        both = jnp.concatenate([high, low], axis=0)
        router_grads = dot_float(both, xg[:, :width])
        drouter_ref[...] = router_grads[:EXPERTS] + router_grads[EXPERTS:]
        padded = jnp.concatenate(
            [grad_logits, jnp.zeros((128 - EXPERTS, group), F32)], axis=0
        )
        glt_scr[...] = padded.T.astype(BF)
        for s in range(tp):
            start = pl.multiple_of(pos_ref[s] * own, own)
            rows_x = xg[pl.ds(start, own), :width]
            rows_g = xg[pl.ds(start, own), width:]
            gate_part = dot_float(rows_x, w_scr[0])
            up_part = dot_float(rows_x, w_scr[1])
            sig = jax.nn.sigmoid(gate_part)
            act = gate_part * sig
            hidden = (act * up_part).astype(BF)
            grad_hid = dot_float(rows_g, w_scr[2])
            d_gate = (grad_hid * up_part * sig * (1.0 + gate_part * (1.0 - sig))).astype(BF)
            d_up = (grad_hid * act).astype(BF)
            act_scr[pl.ds(start, own), :ff] = d_gate
            act_scr[pl.ds(start, own), ff : 2 * ff] = d_up
            act_scr[pl.ds(start, own), 2 * ff :] = hidden
            cols = col_ref[pl.ds(start, own), :]
            slot_ids = lax.broadcasted_iota(jnp.int32, (own, slots), 1)
            pick = jnp.where(
                (cols[:, 0:1] == slot_ids) | (cols[:, 1:2] == slot_ids), 1.0, 0.0
            ).astype(BF)
            branch_refs[s][...] = (
                dot_right_t(hidden, w_scr[2]) + dot_float(pick, y_scr[:, :width])
            ).astype(BF)
            routed = dot_float(glt_scr[pl.ds(start, own), :], router_ref[...])
            dffn_refs[s][...] = (
                dot_right_t(d_gate, w_scr[0])
                + dot_right_t(d_up, w_scr[1])
                + dot_float(pick, y_scr[:, width:])
                + routed
            ).astype(BF)
        dw_scr[0] = dot_left_t(xg[:, :width], act_scr[:, :ff])
        dw_scr[1] = dot_left_t(xg[:, :width], act_scr[:, ff : 2 * ff])
        dw_scr[2] = dot_left_t(xg[:, width:], act_scr[:, 2 * ff :])
        store_grads()


def moe(tp, positions, idx_rows, idx_cols, router_rows, ffn, grads, wa, wb):
    np = len(wa)
    own, width = ffn[0].shape
    group = own * tp
    mats, _, rows, half = wa[0].shape
    whole = pl.BlockSpec(index_map=lambda e, p: (0, 0))
    full = lambda a: pl.BlockSpec(a.shape, lambda e, p: (0, 0))
    piece = pl.BlockSpec((None, 3, rows, half), lambda e, p: (e, 0, 0, 0))
    tok = pl.BlockSpec((own, width), lambda e, p: (0, 0))
    out_shape = (
        [jax.ShapeDtypeStruct((own, width), BF)] * (2 * tp)
        + [jax.ShapeDtypeStruct((EXPERTS, width), F32)]
        + [jax.ShapeDtypeStruct(wa[0].shape, BF)] * (2 * np)
    )
    outs = pl.pallas_call(
        functools.partial(moe_body, tp, np, rows),
        out_shape=out_shape,
        grid_spec=pltpu.PrefetchScalarGridSpec(
            num_scalar_prefetch=1,
            grid=(EXPERTS + 1,),
            in_specs=[full(idx_rows), full(idx_cols), full(router_rows)]
            + [tok] * (2 * tp)
            + [piece] * (2 * np),
            out_specs=[tok] * (2 * tp)
            + [pl.BlockSpec((EXPERTS, width), lambda e, p: (0, 0))]
            + [piece] * (2 * np),
            scratch_shapes=[
                pltpu.VMEM((group, 2 * width), BF),
                pltpu.VMEM((3, width, 2 * half), BF),
                pltpu.VMEM((3, width, 2 * half), F32),
                pltpu.VMEM((EXPERTS * CAP, 2 * width), BF),
                pltpu.VMEM((8, group), F32),
                pltpu.VMEM((8, group), F32),
                pltpu.VMEM((group, 128), BF),
                pltpu.VMEM((group, 6 * half), BF),
            ],
        ),
        compiler_params=pltpu.CompilerParams(
            dimension_semantics=("arbitrary",), vmem_limit_bytes=60 * 1024 * 1024
        ),
        name="moe",
    )(positions, idx_rows, idx_cols, router_rows, *ffn, *grads, *wa, *wb)
    return (
        outs[:tp],
        outs[tp : 2 * tp],
        outs[2 * tp],
        outs[2 * tp + 1 : 2 * tp + 1 + np],
        outs[2 * tp + 1 + np :],
    )


def shards(
    n,
    tp,
    tokens,
    cotangent,
    seq_lengths,
    expert_routes,
    expert_slots,
    attn_gain,
    ffn_gain,
    router_weight,
    query_weight,
    key_weight,
    value_weight,
    out_weight,
    shared_gate,
    shared_up,
    shared_down,
    expert_gate,
    expert_up,
    expert_down,
):
    own_rows, width = tokens.shape
    t_own = lax.axis_index("tp")
    f_own = lax.axis_index("fsdp")
    piece_rows = query_weight.shape[0]
    cube = n & (n - 1) == 0 and 4 <= n <= 8 and piece_rows % 16 == 0
    bits = [1 << b for b in range(n.bit_length() - 1)]
    order_a = bits[1:] + bits[:1]
    order_b = bits[1:][::-1] + bits[:1]

    def shift(value, s):
        return lax.ppermute(value, "tp", [(i, (i + s) % tp) for i in range(tp)])

    def flip(value, k):
        return lax.ppermute(value, "fsdp", [(i, i ^ k) for i in range(n)])

    def tp_gather(value):
        return [value] + [shift(value, tp - s) for s in range(1, tp)]

    def tp_scatter(pieces):
        total = pieces[0].astype(F32)
        for s in range(1, tp):
            total = total + shift(pieces[s], s).astype(F32)
        return total

    def fs_gather(held, order):
        for k in order:
            held = dict(held)
            held.update({i | k: flip(held[i], k) for i in list(held)})
        return held

    def fs_scatter(held, order):
        for k in order:
            low = [i for i in held if not i & k]
            got = {i: flip(held[i | k], k) for i in low}
            held = {i: held[i].astype(F32) + got[i].astype(F32) for i in low}
            if len(low) > 1:
                held = {i: v.astype(BF) for i, v in held.items()}
        return held

    def listed(held):
        return [held[i] for i in range(len(held))]

    def whole_gather(value, axis):
        return [lax.all_gather(value, "fsdp", axis=axis, tiled=True)]

    def whole_scatter(value, axis):
        summed = lax.psum_scatter(value, "fsdp", scatter_dimension=axis, tiled=True)
        return summed.astype(F32)

    tie = lax.optimization_barrier

    tp_pos = (t_own + jnp.arange(tp, dtype=jnp.int32)) % tp
    if cube:
        fs_pos = f_own ^ jnp.arange(n, dtype=jnp.int32)
    else:
        fs_pos = jnp.zeros((1,), jnp.int32)
    positions = jnp.concatenate([tp_pos, fs_pos])

    gain_len = attn_gain.shape[0]
    packed_gains = jnp.concatenate(
        [
            router_weight,
            attn_gain[:, None],
            ffn_gain[:, None],
            jnp.zeros((gain_len, PACK - EXPERTS - 2), BF),
        ],
        axis=1,
    )
    gain_pieces = tp_gather(packed_gains)
    gain_rows = jnp.concatenate(gain_pieces + gain_pieces[:-1], axis=0)
    gain_rows = lax.dynamic_slice_in_dim(
        gain_rows, ((tp - t_own) % tp) * gain_len, piece_rows, 0
    )
    token_pieces = tp_gather(tokens)
    att_cols = query_weight.shape[1]
    attn_pack = jnp.concatenate([query_weight, key_weight, value_weight, out_weight.T], axis=1)
    stacked = jnp.stack(
        [
            jnp.concatenate([expert_gate, shared_gate[None]], axis=0),
            jnp.concatenate([expert_up, shared_up[None]], axis=0),
            jnp.concatenate([expert_down, shared_down[None]], axis=0).transpose(0, 2, 1),
        ],
        axis=1,
    )
    half = stacked.shape[-1] // 2
    held_a, held_b = stacked[..., :half], stacked[..., half:]
    if cube:
        pack_pieces = listed(fs_gather({0: attn_pack}, order_a))
        gain_pieces = listed(fs_gather({0: gain_rows}, order_a))
        pack_pieces, held_a, held_b = tie((pack_pieces, held_a, held_b))
        held_a = fs_gather({0: held_a}, order_a[:1])
        held_b = fs_gather({0: held_b}, order_b[:1])
    else:
        pack_pieces = whole_gather(attn_pack, 0)
        gain_pieces = whole_gather(gain_rows, 0)

    offset = t_own * own_rows
    row_place = offset + lax.iota(jnp.int32, own_rows)
    live_rows = (row_place < seq_lengths[0]).astype(F32)[:, None]
    grad_out = live_rows * cotangent.astype(F32)
    grad_own = grad_out.astype(BF)
    token_pieces, grad_own = tie((token_pieces, grad_own))
    grad_pieces = tp_gather(grad_own)

    attn_parts, saved = attn_fwd(tp, positions, seq_lengths, token_pieces, pack_pieces, gain_pieces)
    attn_parts, grad_pieces, held_a, held_b = tie((attn_parts, grad_pieces, held_a, held_b))
    small = saved[7]
    gain_attn = small[EXPERTS].astype(F32)
    gain_ffn = small[EXPERTS + 1].astype(F32)
    rows_in = tokens.astype(F32)
    residual = rows_in + tp_scatter(attn_parts)
    normed_ffn, inverse_ffn = norm_apply(residual, gain_ffn)
    ffn_pieces = tp_gather(normed_ffn.astype(BF))
    if cube:
        weights_a = listed(fs_gather(held_a, order_a[1:]))
        weights_b = listed(fs_gather(held_b, order_b[1:]))
    else:
        weights_a, weights_b = whole_gather(held_a, 2), whole_gather(held_b, 2)

    flat = expert_routes * CAP + expert_slots
    idx_rows = jnp.concatenate(
        [flat.T, expert_routes.T, jnp.zeros((4, flat.shape[0]), jnp.int32)], axis=0
    )
    branch_pieces, dffn_pieces, router_grad, grads_a, grads_b = moe(
        tp, positions, idx_rows, flat, small, ffn_pieces, grad_pieces, weights_a, weights_b
    )
    grad_ffn_own = tp_scatter(dffn_pieces)
    if cube:
        held_a = fs_scatter(dict(enumerate(grads_a)), order_a[-1:])
        held_b = fs_scatter(dict(enumerate(grads_b)), order_b[-1:])
        grad_ffn_own, held_a, held_b = tie((grad_ffn_own, held_a, held_b))
        held_a = fs_scatter(held_a, order_a[1:-1])
        held_b = fs_scatter(held_b, order_b[1:-1])
    grad_residual_norm, ffn_gain_grad = norm_back(residual, inverse_ffn, gain_ffn, grad_ffn_own)
    grad_residual = grad_out + grad_residual_norm
    res_pieces = tp_gather(grad_residual.astype(BF))
    res_pieces, branch_pieces = tie((res_pieces, branch_pieces))
    branch_own = tp_scatter(branch_pieces)
    layer_out = (live_rows * (residual + branch_own)).astype(BF)
    normed_parts, dpack, attn_gain_grad = attn_bwd(
        tp, len(pack_pieces), positions, seq_lengths, res_pieces, saved
    )
    normed_parts, layer_out, held_a, held_b = tie((normed_parts, layer_out, held_a, held_b))
    small_grads = jnp.concatenate(
        [router_grad, attn_gain_grad, ffn_gain_grad[None], jnp.zeros((6, width), F32)], axis=0
    )
    for_sum = [small_grads] + [shift(small_grads, s) for s in range(1, tp)]
    small_grads = functools.reduce(lambda u, v: u + v, for_sum)
    if cube:
        for_sum = [small_grads] + [flip(small_grads, k) for k in range(1, n)]
        small_grads = functools.reduce(lambda u, v: u + v, for_sum)
    else:
        small_grads = lax.psum(small_grads, "fsdp")
    small_own = lax.dynamic_slice_in_dim(
        small_grads, (f_own * tp + t_own) * gain_len, gain_len, 1
    )
    grad_attn_own = tp_scatter(normed_parts)
    inverse_attn = lax.rsqrt(jnp.mean(rows_in * rows_in, axis=-1, keepdims=True) + EPSILON)
    grad_tokens = grad_residual + norm_back(rows_in, inverse_attn, gain_attn, grad_attn_own)[0]
    if cube:
        pack_own = fs_scatter(dict(enumerate(dpack)), order_a[::-1])[0]
        grads_a = fs_scatter(held_a, order_a[:1])[0]
        grads_b = fs_scatter(held_b, order_b[:1])[0]
    else:
        pack_own = whole_scatter(dpack[0], 0)
        grads_a, grads_b = whole_scatter(grads_a[0], 2), whole_scatter(grads_b[0], 2)
    own_grads = jnp.concatenate([grads_a, grads_b], axis=-1)
    return (
        layer_out,
        grad_tokens,
        small_own[EXPERTS],
        small_own[EXPERTS + 1],
        small_own[:EXPERTS].T,
        pack_own[:, :att_cols],
        pack_own[:, att_cols : 2 * att_cols],
        pack_own[:, 2 * att_cols : 3 * att_cols],
        pack_own[:, 3 * att_cols : 4 * att_cols].T,
        own_grads[EXPERTS, 0],
        own_grads[EXPERTS, 1],
        own_grads[EXPERTS, 2].T,
        own_grads[:EXPERTS, 0],
        own_grads[:EXPERTS, 1],
        own_grads[:EXPERTS, 2].transpose(0, 2, 1),
    )


def solution(mesh):
    placed = (
        P(("fsdp", "tp"), None),
        P(("fsdp", "tp"), None),
        P("fsdp"),
        P("fsdp", None),
        P("fsdp", None),
        P(("fsdp", "tp")),
        P(("fsdp", "tp")),
        P(("fsdp", "tp"), None),
        P("fsdp", "tp"),
        P("fsdp", "tp"),
        P("fsdp", "tp"),
        P("tp", "fsdp"),
        P("fsdp", "tp"),
        P("fsdp", "tp"),
        P("tp", "fsdp"),
        P(None, "fsdp", "tp"),
        P(None, "fsdp", "tp"),
        P(None, "tp", "fsdp"),
    )
    return jax.shard_map(
        functools.partial(shards, mesh.shape["fsdp"], mesh.shape["tp"]),
        mesh=mesh,
        in_specs=placed,
        out_specs=(
            P(("fsdp", "tp"), None),
            P(("fsdp", "tp"), None),
            P(("fsdp", "tp")),
            P(("fsdp", "tp")),
            P(("fsdp", "tp"), None),
            P("fsdp", "tp"),
            P("fsdp", "tp"),
            P("fsdp", "tp"),
            P("tp", "fsdp"),
            P("fsdp", "tp"),
            P("fsdp", "tp"),
            P("tp", "fsdp"),
            P(None, "fsdp", "tp"),
            P(None, "fsdp", "tp"),
            P(None, "tp", "fsdp"),
        ),
        check_vma=False,
    )
```

```python
import functools

import jax
import jax.numpy as jnp
from jax import lax
from jax.experimental import pallas as pl
from jax.experimental.pallas import tpu as pltpu
from jax.sharding import PartitionSpec as P


HD = 64
EXPERTS = 8
CAP = 320
EPSILON = 1e-06
MASKED_SCORE = -1e30
BF = jnp.bfloat16
F32 = jnp.float32
PACK = 128


def dot_float(left_mat, right_mat):
    return jnp.dot(left_mat, right_mat, preferred_element_type=F32)


def dot_left_t(left_mat, right_mat):
    return lax.dot_general(left_mat, right_mat, (((0,), (0,)), ((), ())), preferred_element_type=F32)


def dot_right_t(left_mat, right_mat):
    return lax.dot_general(left_mat, right_mat, (((1,), (1,)), ((), ())), preferred_element_type=F32)


def norm_apply(rows_in, gain_row):
    inverse = lax.rsqrt(jnp.mean(rows_in * rows_in, axis=-1, keepdims=True) + EPSILON)
    return (rows_in * inverse * gain_row, inverse)


def norm_back(rows_in, inverse, gain_row, upstream):
    scaled = upstream * gain_row
    gain_grad = jnp.sum(upstream * rows_in * inverse, axis=0)
    rows_grad = inverse * scaled - rows_in * inverse**3 * jnp.mean(
        scaled * rows_in, axis=-1, keepdims=True
    )
    return (rows_grad, gain_grad)


def attn_fwd_body(tp, np, pos_ref, len_ref, *refs):
    x_refs, refs = refs[:tp], refs[tp:]
    pack_refs, gain_refs, refs = refs[:np], refs[np : 2 * np], refs[2 * np :]
    part_refs, refs = refs[:tp], refs[tp:]
    rows_ref, q_ref, k_ref, v_ref, att_ref, lse_ref, w_ref, small_ref, gain_scr = refs
    own, _ = x_refs[0].shape
    heads = q_ref.shape[0]
    att_width = heads * HD
    prow = pack_refs[0].shape[0]
    for j in range(np):
        start = pl.multiple_of(pos_ref[tp + j] * prow, prow)
        w_ref[pl.ds(start, prow), :] = pack_refs[j][...]
        gain_scr[pl.ds(start, prow), :] = gain_refs[j][...].astype(F32)
    small = gain_scr[...].T
    small_ref[...] = small.astype(BF)
    gain = small[EXPERTS : EXPERTS + 1, :]
    for s in range(tp):
        start = pl.multiple_of(pos_ref[s] * own, own)
        rows = norm_apply(x_refs[s][...].astype(F32), gain)[0].astype(BF)
        rows_ref[pl.ds(start, own), :] = rows
        qkv = dot_float(rows, w_ref[:, : 3 * att_width]).astype(BF)
        for h in range(heads):
            for m, ref in enumerate((q_ref, k_ref, v_ref)):
                ref[h, pl.ds(start, own), :] = qkv[:, m * att_width + h * HD :][:, :HD]
    length = len_ref[0]
    for h in range(heads):
        for i in range(tp):
            ext = (i + 1) * own
            probs, row_max, total = None, None, None
            scores = masked(q_ref[h, i * own : ext, :], k_ref[h, :ext, :], length, i * own)
            row_max = jnp.max(scores, axis=-1, keepdims=True)
            exp_scores = jnp.exp(scores - row_max)
            total = jnp.sum(exp_scores, axis=-1, keepdims=True)
            probs = (exp_scores * (1.0 / total)).astype(BF)
            att_ref[i * own : ext, h * HD : (h + 1) * HD] = dot_float(
                probs, v_ref[h, :ext, :]
            ).astype(BF)
            lse_ref[i * own : ext, h : h + 1] = row_max + jnp.log(total)
    for s in range(tp):
        start = pl.multiple_of(pos_ref[s] * own, own)
        part_refs[s][...] = dot_right_t(
            att_ref[pl.ds(start, own), :], w_ref[:, 3 * att_width :]
        ).astype(BF)


def masked(query_rows, key_rows, length, first):
    scores = dot_right_t(query_rows, key_rows) * HD ** (-0.5)
    row_pos = lax.broadcasted_iota(jnp.int32, scores.shape, 0) + first
    col_pos = lax.broadcasted_iota(jnp.int32, scores.shape, 1)
    return jnp.where((col_pos <= row_pos) & (col_pos < length), scores, MASKED_SCORE)


def attn_fwd(tp, positions, length, x_pieces, pack_pieces, gain_pieces):
    np = len(pack_pieces)
    own, width = x_pieces[0].shape
    group = own * tp
    att_width = pack_pieces[0].shape[1] // 4
    heads = att_width // HD
    shape = jax.ShapeDtypeStruct
    outs = pl.pallas_call(
        functools.partial(attn_fwd_body, tp, np),
        out_shape=[shape((own, width), BF)] * tp
        + [shape((group, width), BF)]
        + [shape((heads, group, HD), BF)] * 3
        + [
            shape((group, att_width), BF),
            shape((group, 128), F32),
            shape((width, 4 * att_width), BF),
            shape((PACK, width), BF),
        ],
        in_specs=[pl.BlockSpec(memory_space=pltpu.SMEM)] * 2
        + [pl.BlockSpec(memory_space=pltpu.VMEM)] * (tp + 2 * np),
        out_specs=[pl.BlockSpec(memory_space=pltpu.VMEM)] * (tp + 8),
        scratch_shapes=[pltpu.VMEM((width, PACK), F32)],
        compiler_params=pltpu.CompilerParams(vmem_limit_bytes=56 * 1024 * 1024),
        name="attn_fwd",
    )(positions, length, *x_pieces, *pack_pieces, *gain_pieces)
    return outs[:tp], outs[tp:]


def attn_bwd_body(tp, np, pos_ref, len_ref, *refs):
    g_refs, refs = refs[:tp], refs[tp:]
    rows_ref, q_ref, k_ref, v_ref, att_ref, lse_ref, w_ref, small_ref = refs[:8]
    refs = refs[8:]
    part_refs, refs = refs[:tp], refs[tp:]
    dpack_refs, refs = refs[:np], refs[np:]
    dgain_ref, gres, g_scr, ga_scr, dk_scr, dv_scr, dw_scr = refs
    own, width = g_refs[0].shape
    heads = q_ref.shape[0]
    att_width = heads * HD
    prow = dpack_refs[0].shape[0]
    for s in range(tp):
        start = pl.multiple_of(pos_ref[s] * own, own)
        gres[pl.ds(start, own), :] = g_refs[s][...]
    grad_att = dot_float(gres[...], w_ref[:, 3 * att_width :]).astype(BF)
    for h in range(heads):
        ga_scr[h] = grad_att[:, h * HD : (h + 1) * HD]
    dw_scr[:, 3 * att_width :] = dot_left_t(gres[...], att_ref[...])
    length = len_ref[0]
    factor = HD ** (-0.5)
    for h in range(heads):
        dk_scr[...] = jnp.zeros_like(dk_scr)
        dv_scr[...] = jnp.zeros_like(dv_scr)
        for i in range(tp):
            ext = (i + 1) * own
            q_rows = q_ref[h, i * own : ext, :]
            ga_rows = ga_scr[h, i * own : ext, :]
            scores = masked(q_rows, k_ref[h, :ext, :], length, i * own)
            probs = jnp.exp(scores - lse_ref[i * own : ext, h : h + 1])
            grad_probs = dot_right_t(ga_rows, v_ref[h, :ext, :])
            inner = jnp.sum(probs * grad_probs, axis=-1, keepdims=True)
            grad_scores = (probs * (grad_probs - inner)).astype(BF)
            g_scr[i * own : ext, h * HD : (h + 1) * HD] = (
                dot_float(grad_scores, k_ref[h, :ext, :]) * factor
            ).astype(BF)
            dk_scr[:ext, :] += dot_left_t(grad_scores, q_rows)
            dv_scr[:ext, :] += dot_left_t(probs.astype(BF), ga_rows)
        g_scr[:, att_width + h * HD : att_width + (h + 1) * HD] = (dk_scr[...] * factor).astype(BF)
        g_scr[:, 2 * att_width + h * HD : 2 * att_width + (h + 1) * HD] = dv_scr[...].astype(BF)
    dgain = jnp.zeros((1, width), F32)
    for s in range(tp):
        start = pl.multiple_of(pos_ref[s] * own, own)
        grad_rows = dot_right_t(g_scr[pl.ds(start, own), :], w_ref[:, : 3 * att_width])
        part_refs[s][...] = grad_rows.astype(BF)
        dgain = dgain + jnp.sum(
            grad_rows * rows_ref[pl.ds(start, own), :].astype(F32), axis=0, keepdims=True
        )
    dgain_ref[...] = dgain / small_ref[EXPERTS : EXPERTS + 1, :].astype(F32)
    dw_scr[:, : 3 * att_width] = dot_left_t(rows_ref[...], g_scr[...])
    for j in range(np):
        start = pl.multiple_of(pos_ref[tp + j] * prow, prow)
        dpack_refs[j][...] = dw_scr[pl.ds(start, prow), :].astype(BF)


def attn_bwd(tp, np, positions, length, g_pieces, saved):
    own, width = g_pieces[0].shape
    group = own * tp
    heads = saved[1].shape[0]
    att_width = heads * HD
    shape = jax.ShapeDtypeStruct
    outs = pl.pallas_call(
        functools.partial(attn_bwd_body, tp, np),
        out_shape=[shape((own, width), BF)] * tp
        + [shape((width // np, 4 * att_width), BF)] * np
        + [shape((1, width), F32)],
        in_specs=[pl.BlockSpec(memory_space=pltpu.SMEM)] * 2
        + [pl.BlockSpec(memory_space=pltpu.VMEM)] * (tp + 8),
        out_specs=[pl.BlockSpec(memory_space=pltpu.VMEM)] * (tp + np + 1),
        scratch_shapes=[
            pltpu.VMEM((group, width), BF),
            pltpu.VMEM((group, 3 * att_width), BF),
            pltpu.VMEM((heads, group, HD), BF),
            pltpu.VMEM((group, HD), F32),
            pltpu.VMEM((group, HD), F32),
            pltpu.VMEM((width, 4 * att_width), F32),
        ],
        compiler_params=pltpu.CompilerParams(vmem_limit_bytes=56 * 1024 * 1024),
        name="attn_bwd",
    )(positions, length, *g_pieces, *saved)
    return outs[:tp], outs[tp : tp + np], outs[tp + np]


def moe_body(tp, np, rows, pos_ref, idx_ref, col_ref, router_ref, *refs):
    ffn_refs = refs[:tp]
    grad_refs = refs[tp : 2 * tp]
    refs = refs[2 * tp :]
    wa_refs = refs[:np]
    wb_refs = refs[np : 2 * np]
    refs = refs[2 * np :]
    branch_refs = refs[:tp]
    dffn_refs = refs[tp : 2 * tp]
    drouter_ref = refs[2 * tp]
    refs = refs[2 * tp + 1 :]
    da_refs = refs[:np]
    db_refs = refs[np : 2 * np]
    xg, w_scr, dw_scr, y_scr, gate_scr, gg_scr, glt_scr, act_scr = refs[2 * np :]
    step = pl.program_id(0)
    own = ffn_refs[0].shape[0]
    width = ffn_refs[0].shape[1]
    group = own * tp
    half = wa_refs[0].shape[-1]
    ff = 2 * half
    slots = EXPERTS * CAP

    @pl.when(step == 0)
    def _():
        for s in range(tp):
            start = pl.multiple_of(pos_ref[s] * own, own)
            xg[pl.ds(start, own), :width] = ffn_refs[s][...]
            xg[pl.ds(start, own), width:] = grad_refs[s][...]
        logits = dot_right_t(router_ref[...], xg[:, :width])[:EXPERTS]
        ids = lax.broadcasted_iota(jnp.int32, (EXPERTS, group), 0)
        gap = jnp.sum(
            jnp.where(idx_ref[2:3, :] == ids, logits, 0.0)
            - jnp.where(idx_ref[3:4, :] == ids, logits, 0.0),
            axis=0,
            keepdims=True,
        )
        gate_scr[0:1, :] = jax.nn.sigmoid(gap)
        gate_scr[1:2, :] = jax.nn.sigmoid(-gap)
        gg_scr[...] = jnp.zeros_like(gg_scr)

    for m in range(3):
        for j in range(np):
            start = pl.multiple_of(pos_ref[tp + j] * rows, rows)
            w_scr[m, pl.ds(start, rows), :half] = wa_refs[j][m]
            w_scr[m, pl.ds(start, rows), half:] = wb_refs[j][m]

    def store_grads():
        for m in range(3):
            for j in range(np):
                start = pl.multiple_of(pos_ref[tp + j] * rows, rows)
                da_refs[j][m] = dw_scr[m, pl.ds(start, rows), :half].astype(BF)
                db_refs[j][m] = dw_scr[m, pl.ds(start, rows), half:].astype(BF)

    @pl.when(step < EXPERTS)
    def _():
        ids = lax.broadcasted_iota(jnp.int32, (CAP, group), 0) + step * CAP
        first = idx_ref[0:1, :] == ids
        second = idx_ref[1:2, :] == ids
        pick = jnp.where(first | second, 1.0, 0.0).astype(BF)
        slot_gate = jnp.sum(
            jnp.where(first, gate_scr[0:1, :], jnp.where(second, gate_scr[1:2, :], 0.0)),
            axis=1,
            keepdims=True,
        )
        disp = dot_float(pick, xg[:, :width]).astype(BF)
        grad_rows = dot_float(pick, xg[:, width:])
        gate_part = dot_float(disp, w_scr[0])
        up_part = dot_float(disp, w_scr[1])
        sig = jax.nn.sigmoid(gate_part)
        act = gate_part * sig
        hidden = (act * up_part).astype(BF)
        rows_out = dot_right_t(hidden, w_scr[2])
        slot_grad = jnp.sum(grad_rows * rows_out, axis=1, keepdims=True)
        gg_scr[0:1, :] += jnp.sum(jnp.where(first, slot_grad, 0.0), axis=0, keepdims=True)
        gg_scr[1:2, :] += jnp.sum(jnp.where(second, slot_grad, 0.0), axis=0, keepdims=True)
        grad_exp = (slot_gate * grad_rows).astype(BF)
        grad_hid = dot_float(grad_exp, w_scr[2])
        d_gate = (grad_hid * up_part * sig * (1.0 + gate_part * (1.0 - sig))).astype(BF)
        d_up = (grad_hid * act).astype(BF)
        grad_disp = dot_right_t(d_gate, w_scr[0]) + dot_right_t(d_up, w_scr[1])
        base = pl.multiple_of(step * CAP, CAP)
        y_scr[pl.ds(base, CAP), :width] = (slot_gate * rows_out).astype(BF)
        y_scr[pl.ds(base, CAP), width:] = grad_disp.astype(BF)
        dw_scr[0] = dot_left_t(disp, d_gate)
        dw_scr[1] = dot_left_t(disp, d_up)
        dw_scr[2] = dot_left_t(grad_exp, hidden)
        store_grads()

    @pl.when(step == EXPERTS)
    def _():
        ids = lax.broadcasted_iota(jnp.int32, (EXPERTS, group), 0)
        change = (gg_scr[0:1, :] - gg_scr[1:2, :]) * gate_scr[0:1, :] * gate_scr[1:2, :]
        grad_logits = jnp.where(idx_ref[2:3, :] == ids, change, 0.0) - jnp.where(
            idx_ref[3:4, :] == ids, change, 0.0
        )
        high = grad_logits.astype(BF)
        low = (grad_logits - high.astype(F32)).astype(BF)
        both = jnp.concatenate([high, low], axis=0)
        router_grads = dot_float(both, xg[:, :width])
        drouter_ref[...] = router_grads[:EXPERTS] + router_grads[EXPERTS:]
        padded = jnp.concatenate(
            [grad_logits, jnp.zeros((128 - EXPERTS, group), F32)], axis=0
        )
        glt_scr[...] = padded.T.astype(BF)
        for s in range(tp):
            start = pl.multiple_of(pos_ref[s] * own, own)
            rows_x = xg[pl.ds(start, own), :width]
            rows_g = xg[pl.ds(start, own), width:]
            gate_part = dot_float(rows_x, w_scr[0])
            up_part = dot_float(rows_x, w_scr[1])
            sig = jax.nn.sigmoid(gate_part)
            act = gate_part * sig
            hidden = (act * up_part).astype(BF)
            grad_hid = dot_float(rows_g, w_scr[2])
            d_gate = (grad_hid * up_part * sig * (1.0 + gate_part * (1.0 - sig))).astype(BF)
            d_up = (grad_hid * act).astype(BF)
            act_scr[pl.ds(start, own), :ff] = d_gate
            act_scr[pl.ds(start, own), ff : 2 * ff] = d_up
            act_scr[pl.ds(start, own), 2 * ff :] = hidden
            cols = col_ref[pl.ds(start, own), :]
            slot_ids = lax.broadcasted_iota(jnp.int32, (own, slots), 1)
            pick = jnp.where(
                (cols[:, 0:1] == slot_ids) | (cols[:, 1:2] == slot_ids), 1.0, 0.0
            ).astype(BF)
            branch_refs[s][...] = (
                dot_right_t(hidden, w_scr[2]) + dot_float(pick, y_scr[:, :width])
            ).astype(BF)
            routed = dot_float(glt_scr[pl.ds(start, own), :], router_ref[...])
            dffn_refs[s][...] = (
                dot_right_t(d_gate, w_scr[0])
                + dot_right_t(d_up, w_scr[1])
                + dot_float(pick, y_scr[:, width:])
                + routed
            ).astype(BF)
        dw_scr[0] = dot_left_t(xg[:, :width], act_scr[:, :ff])
        dw_scr[1] = dot_left_t(xg[:, :width], act_scr[:, ff : 2 * ff])
        dw_scr[2] = dot_left_t(xg[:, width:], act_scr[:, 2 * ff :])
        store_grads()


def moe(tp, positions, idx_rows, idx_cols, router_rows, ffn, grads, wa, wb):
    np = len(wa)
    own, width = ffn[0].shape
    group = own * tp
    _, _, rows, half = wa[0].shape
    whole = pl.BlockSpec(index_map=lambda e, p: (0, 0))
    full = lambda a: pl.BlockSpec(a.shape, lambda e, p: (0, 0))
    piece = pl.BlockSpec((None, 3, rows, half), lambda e, p: (e, 0, 0, 0))
    tok = pl.BlockSpec((own, width), lambda e, p: (0, 0))
    out_shape = (
        [jax.ShapeDtypeStruct((own, width), BF)] * (2 * tp)
        + [jax.ShapeDtypeStruct((EXPERTS, width), F32)]
        + [jax.ShapeDtypeStruct(wa[0].shape, BF)] * (2 * np)
    )
    outs = pl.pallas_call(
        functools.partial(moe_body, tp, np, rows),
        out_shape=out_shape,
        grid_spec=pltpu.PrefetchScalarGridSpec(
            num_scalar_prefetch=1,
            grid=(EXPERTS + 1,),
            in_specs=[full(idx_rows), full(idx_cols), full(router_rows)]
            + [tok] * (2 * tp)
            + [piece] * (2 * np),
            out_specs=[tok] * (2 * tp)
            + [pl.BlockSpec((EXPERTS, width), lambda e, p: (0, 0))]
            + [piece] * (2 * np),
            scratch_shapes=[
                pltpu.VMEM((group, 2 * width), BF),
                pltpu.VMEM((3, width, 2 * half), BF),
                pltpu.VMEM((3, width, 2 * half), F32),
                pltpu.VMEM((EXPERTS * CAP, 2 * width), BF),
                pltpu.VMEM((8, group), F32),
                pltpu.VMEM((8, group), F32),
                pltpu.VMEM((group, 128), BF),
                pltpu.VMEM((group, 6 * half), BF),
            ],
        ),
        compiler_params=pltpu.CompilerParams(
            dimension_semantics=("arbitrary",), vmem_limit_bytes=60 * 1024 * 1024
        ),
        name="moe",
    )(positions, idx_rows, idx_cols, router_rows, *ffn, *grads, *wa, *wb)
    return (
        outs[:tp],
        outs[tp : 2 * tp],
        outs[2 * tp],
        outs[2 * tp + 1 : 2 * tp + 1 + np],
        outs[2 * tp + 1 + np :],
    )


def shards(
    n,
    tp,
    tokens,
    cotangent,
    seq_lengths,
    expert_routes,
    expert_slots,
    attn_gain,
    ffn_gain,
    router_weight,
    query_weight,
    key_weight,
    value_weight,
    out_weight,
    shared_gate,
    shared_up,
    shared_down,
    expert_gate,
    expert_up,
    expert_down,
):
    own_rows, width = tokens.shape
    t_own = lax.axis_index("tp")
    f_own = lax.axis_index("fsdp")
    piece_rows = query_weight.shape[0]
    cube = n & (n - 1) == 0 and 4 <= n <= 8 and piece_rows % 16 == 0
    bits = [1 << b for b in range(n.bit_length() - 1)]
    order_a = bits[1:] + bits[:1]
    order_b = bits[1:][::-1] + bits[:1]

    def shift(value, s):
        return lax.ppermute(value, "tp", [(i, (i + s) % tp) for i in range(tp)])

    def flip(value, k):
        return lax.ppermute(value, "fsdp", [(i, i ^ k) for i in range(n)])

    def tp_gather(value):
        return [value] + [shift(value, tp - s) for s in range(1, tp)]

    def tp_scatter(pieces):
        total = pieces[0].astype(F32)
        for s in range(1, tp):
            total = total + shift(pieces[s], s).astype(F32)
        return total

    def fs_gather(held, order):
        for k in order:
            held = dict(held)
            held.update({i | k: flip(held[i], k) for i in list(held)})
        return held

    def fs_send(held, k):
        return {i: flip(held[i | k], k) for i in held if not i & k}

    def fs_add(held, got):
        held = {i: held[i].astype(F32) + got[i].astype(F32) for i in got}
        if len(held) > 1:
            held = {i: v.astype(BF) for i, v in held.items()}
        return held

    def fs_scatter(held, order):
        for k in order:
            held = fs_add(held, fs_send(held, k))
        return held

    def after(value, first):
        return tie((value, first))[0]

    def listed(held):
        return [held[i] for i in range(len(held))]

    def whole_gather(value, axis):
        return [lax.all_gather(value, "fsdp", axis=axis, tiled=True)]

    def whole_scatter(value, axis):
        summed = lax.psum_scatter(value, "fsdp", scatter_dimension=axis, tiled=True)
        return summed.astype(F32)

    tie = lax.optimization_barrier

    tp_pos = (t_own + jnp.arange(tp, dtype=jnp.int32)) % tp
    if cube:
        fs_pos = f_own ^ jnp.arange(n, dtype=jnp.int32)
    else:
        fs_pos = jnp.zeros((1,), jnp.int32)
    positions = jnp.concatenate([tp_pos, fs_pos])

    gain_len = attn_gain.shape[0]
    packed_gains = jnp.concatenate(
        [
            router_weight,
            attn_gain[:, None],
            ffn_gain[:, None],
            jnp.zeros((gain_len, PACK - EXPERTS - 2), BF),
        ],
        axis=1,
    )
    gain_pieces = tp_gather(packed_gains)
    gain_rows = jnp.concatenate(gain_pieces + gain_pieces[:-1], axis=0)
    gain_rows = lax.dynamic_slice_in_dim(
        gain_rows, ((tp - t_own) % tp) * gain_len, piece_rows, 0
    )
    token_pieces = tp_gather(tokens)
    att_cols = query_weight.shape[1]
    attn_pack = jnp.concatenate([query_weight, key_weight, value_weight, out_weight.T], axis=1)
    stacked = jnp.stack(
        [
            jnp.concatenate([expert_gate, shared_gate[None]], axis=0),
            jnp.concatenate([expert_up, shared_up[None]], axis=0),
            jnp.concatenate([expert_down, shared_down[None]], axis=0).transpose(0, 2, 1),
        ],
        axis=1,
    )
    half = stacked.shape[-1] // 2
    held_a, held_b = stacked[..., :half], stacked[..., half:]
    if cube:
        pack_pieces = listed(fs_gather({0: attn_pack}, order_a))
        gain_pieces = listed(fs_gather({0: gain_rows}, order_a))
        pack_pieces, gain_pieces, held_a, held_b = tie((pack_pieces, gain_pieces, held_a, held_b))
        held_a = fs_gather({0: held_a}, order_a[:1])
        held_b = fs_gather({0: held_b}, order_b[:1])
    else:
        pack_pieces = whole_gather(attn_pack, 0)
        gain_pieces = whole_gather(gain_rows, 0)

    offset = t_own * own_rows
    row_place = offset + lax.iota(jnp.int32, own_rows)
    live_rows = (row_place < seq_lengths[0]).astype(F32)[:, None]
    grad_out = live_rows * cotangent.astype(F32)
    grad_own = grad_out.astype(BF)
    gain_pieces, grad_own = tie((gain_pieces, grad_own))
    grad_pieces = tp_gather(grad_own)

    attn_parts, saved = attn_fwd(tp, positions, seq_lengths, token_pieces, pack_pieces, gain_pieces)
    attn_parts, held_a, held_b = tie((attn_parts, held_a, held_b))
    small = saved[7]
    gain_attn = small[EXPERTS].astype(F32)
    gain_ffn = small[EXPERTS + 1].astype(F32)
    rows_in = tokens.astype(F32)
    attn_own = tp_scatter(attn_parts)
    residual = rows_in + attn_own
    normed_ffn, inverse_ffn = norm_apply(residual, gain_ffn)
    normed_low = normed_ffn.astype(BF)
    ffn_pieces = tp_gather(normed_low)
    if cube:
        held_a = after(fs_gather(held_a, order_a[1:2]), normed_low)
        held_b = after(fs_gather(held_b, order_b[1:2]), normed_low)
        weights_a = listed(fs_gather(held_a, order_a[2:]))
        weights_b = listed(fs_gather(held_b, order_b[2:]))
    else:
        weights_a, weights_b = whole_gather(held_a, 2), whole_gather(held_b, 2)

    flat = expert_routes * CAP + expert_slots
    idx_rows = jnp.concatenate(
        [flat.T, expert_routes.T, jnp.zeros((4, flat.shape[0]), jnp.int32)], axis=0
    )
    branch_pieces, dffn_pieces, router_grad, grads_a, grads_b = moe(
        tp, positions, idx_rows, flat, small, ffn_pieces, grad_pieces, weights_a, weights_b
    )
    if cube:
        held_a, held_b = dict(enumerate(grads_a)), dict(enumerate(grads_b))
        got_a = fs_send(held_a, order_a[-1])
        got_b = fs_send(held_b, order_b[-1])
    grad_ffn_own = tp_scatter(dffn_pieces)
    grad_residual_norm, ffn_gain_grad = norm_back(residual, inverse_ffn, gain_ffn, grad_ffn_own)
    grad_residual = grad_out + grad_residual_norm
    grad_res_low = grad_residual.astype(BF)
    res_pieces = tp_gather(grad_res_low)
    if cube:
        held_a, held_b = fs_add(held_a, got_a), fs_add(held_b, got_b)
        got_a = fs_send(held_a, order_a[1])
        got_b = fs_send(held_b, order_b[1])
        held_a, held_b = fs_add(held_a, got_a), fs_add(held_b, got_b)
    res_pieces, branch_pieces = tie((res_pieces, branch_pieces))
    branch_own = tp_scatter(branch_pieces)
    layer_out = (live_rows * (residual + branch_own)).astype(BF)
    normed_parts, dpack, attn_gain_grad = attn_bwd(
        tp, len(pack_pieces), positions, seq_lengths, res_pieces, saved
    )
    small_grads = jnp.concatenate(
        [router_grad, attn_gain_grad, ffn_gain_grad[None], jnp.zeros((6, width), F32)], axis=0
    )
    for_sum = [small_grads] + [shift(small_grads, s) for s in range(1, tp)]
    grad_attn_own = tp_scatter(normed_parts)
    for_sum = after(for_sum, grad_attn_own)
    small_grads = functools.reduce(lambda u, v: u + v, for_sum)
    if cube:
        for_sum = [small_grads] + [flip(small_grads, k) for k in range(1, n)]
        small_grads = functools.reduce(lambda u, v: u + v, for_sum)
    else:
        small_grads = lax.psum(small_grads, "fsdp")
    small_own = lax.dynamic_slice_in_dim(
        small_grads, (f_own * tp + t_own) * gain_len, gain_len, 1
    )
    inverse_attn = lax.rsqrt(jnp.mean(rows_in * rows_in, axis=-1, keepdims=True) + EPSILON)
    grad_tokens = grad_residual + norm_back(rows_in, inverse_attn, gain_attn, grad_attn_own)[0]
    if cube:
        pack_own = fs_scatter(dict(enumerate(dpack)), order_a[::-1])[0]
        grads_a = fs_scatter(held_a, order_a[:1])[0]
        grads_b = fs_scatter(held_b, order_b[:1])[0]
    else:
        pack_own = whole_scatter(dpack[0], 0)
        grads_a, grads_b = whole_scatter(grads_a[0], 2), whole_scatter(grads_b[0], 2)
    own_grads = jnp.concatenate([grads_a, grads_b], axis=-1)
    return (
        layer_out,
        grad_tokens,
        small_own[EXPERTS],
        small_own[EXPERTS + 1],
        small_own[:EXPERTS].T,
        pack_own[:, :att_cols],
        pack_own[:, att_cols : 2 * att_cols],
        pack_own[:, 2 * att_cols : 3 * att_cols],
        pack_own[:, 3 * att_cols : 4 * att_cols].T,
        own_grads[EXPERTS, 0],
        own_grads[EXPERTS, 1],
        own_grads[EXPERTS, 2].T,
        own_grads[:EXPERTS, 0],
        own_grads[:EXPERTS, 1],
        own_grads[:EXPERTS, 2].transpose(0, 2, 1),
    )


def solution(mesh):
    placed = (
        P(("fsdp", "tp"), None),
        P(("fsdp", "tp"), None),
        P("fsdp"),
        P("fsdp", None),
        P("fsdp", None),
        P(("fsdp", "tp")),
        P(("fsdp", "tp")),
        P(("fsdp", "tp"), None),
        P("fsdp", "tp"),
        P("fsdp", "tp"),
        P("fsdp", "tp"),
        P("tp", "fsdp"),
        P("fsdp", "tp"),
        P("fsdp", "tp"),
        P("tp", "fsdp"),
        P(None, "fsdp", "tp"),
        P(None, "fsdp", "tp"),
        P(None, "tp", "fsdp"),
    )

    def body(*args):
        return shards(mesh.shape["fsdp"], mesh.shape["tp"], *args)

    return jax.shard_map(
        body,
        mesh=mesh,
        in_specs=placed,
        out_specs=(
            P(("fsdp", "tp"), None),
            P(("fsdp", "tp"), None),
            P(("fsdp", "tp")),
            P(("fsdp", "tp")),
            P(("fsdp", "tp"), None),
            P("fsdp", "tp"),
            P("fsdp", "tp"),
            P("fsdp", "tp"),
            P("tp", "fsdp"),
            P("fsdp", "tp"),
            P("fsdp", "tp"),
            P("tp", "fsdp"),
            P(None, "fsdp", "tp"),
            P(None, "fsdp", "tp"),
            P(None, "tp", "fsdp"),
        ),
        check_vma=False,
    )
```
